32 devices in a mesh: groups: 2 (over y), seq: 8 (over z, x), ch: 2 (over core).
Axes of the slice: x: 2, y: 2, z: 4, core: 2. Of those that a mesh axis runs over, the one named last changes fastest.
Arguments:
- tokens: int32 [4096], P(('groups', 'seq')), parts along dimension 0, may hold values from 0 to 3
- nuc_table: bfloat16 [3, 4, 4096], P(None, None, 'ch'), may hold values from -6 to 6
- short_filter: float32 [3, 7, 4096], P(None, None, 'ch'), may hold values from -2 to 2
- mr_filter: float32 [256, 128], P('ch'), may hold values from -0.5 to 0.5
- head_weight: bfloat16 [5, 4096, 256], P(None, 'ch'), may hold values from -0.03125 to 0.03125
Outputs:
- annotation: bfloat16 [4096, 256], P(('groups', 'seq')), parts along dimension 0
The draws below stay inside these ranges and needn't reach their ends.
There are 2 independent parts, one for each index of `groups`. The reference program is written for one: setup_inputs(seed, part) draws one part's arguments, and reference() takes and returns one part's arrays. A program takes and returns all parts, laid end to end along the dimension named above; an argument that names none is the same for every part. Nothing has to cross between parts.
Inputs may be any that keep to these rules, and one draw needn't show every extreme that they name: `tokens`: each entry is a nucleotide letter: 0 A, 1 C, 2 G, 3 T; the complement of a is 3 - a. The letters are integers, so they may cross devices packed several to a 16-bit or wider word without losing anything.
All inputs are finite; a program needn't handle non-finite values.
Results may differ from the reference program's by a relative error of at most 0.0049.
Values may be sent and summed in bfloat16 or wider, within the bound.
No kernel may reach another device: no remote copies, remote signals or barrier semaphores. Data moves between devices by JAX's collectives and lax.ppermute only.
A program may use at most 128 MiB of HBM per device.

```python
import jax
import jax.numpy as jnp
from jax import lax

D = 4096
GROUP = 16
TAPS_SHORT = 7
TAPS_MR = 128
TAPS_HEAD = 5
HEAD_OUT = 256
FILTERS = 256
LENGTH = 2048


def touch_ends(result, key, least, largest):
    shape = result.shape
    spot = [jax.random.randint(jax.random.fold_in(key, axis), (), 0, shape[axis]) for axis in range(len(shape))]
    result = result.at[tuple(spot)].set(least)
    longest = shape.index(max(shape))
    spot[longest] = (spot[longest] + 1) % shape[longest]
    return result.at[tuple(spot)].set(largest)


def shard_levels(key, dims, pieces, least, high):
    level, own = 1.0, jax.random.fold_in(key, 6)
    for position, parts in pieces:
        heights = jnp.exp(jax.random.uniform(jax.random.fold_in(own, position), (parts,), jnp.float32, least / len(pieces), high / len(pieces)))
        level = level * jnp.repeat(heights, dims[position] // parts).reshape([-1 if axis == position else 1 for axis in range(len(dims))])
    return level


def noise(rng, extent, width, bound, split=(), kind=jnp.bfloat16):
    gain = shard_levels(rng, extent, split, -0.22, 0.18) if split else 1.0
    entries = jax.random.normal(rng, extent, jnp.float32) * width * gain
    return jnp.minimum(jnp.maximum(entries, -bound), bound).astype(kind)


def setup_inputs(seed: int = 0, part: int = 0) -> dict:
    keys = jax.random.split(jax.random.key(seed), 6)
    part_keys = jax.random.split(jax.random.fold_in(keys[5], part), 6)
    tokens = touch_ends(jax.random.randint(part_keys[0], (LENGTH,), 0, 4), jax.random.fold_in(part_keys[0], 1), 0, 3).astype(jnp.int32)
    nuc_table = noise(keys[1], (3, 4, D), 1.0, 6.0, ((2, 2),))
    short_filter = noise(keys[2], (3, TAPS_SHORT, D), TAPS_SHORT ** -0.5, 2.0, ((2, 2),), jnp.float32)
    mr_filter = noise(keys[3], (FILTERS, TAPS_MR), TAPS_MR ** -0.5, 0.5, ((0, 2),), jnp.float32)
    head_weight = noise(keys[4], (TAPS_HEAD, D, HEAD_OUT), (2 * TAPS_HEAD * D) ** -0.5, 0.03125, ((1, 2),))
    return dict(tokens=tokens, nuc_table=nuc_table, short_filter=short_filter, mr_filter=mr_filter, head_weight=head_weight)


def causal_taps(stream, short_taps):
    short_len = short_taps.shape[0]
    out_count = stream.shape[1] - short_len + 1
    running = short_taps[0] * stream[:, short_len - 1: short_len - 1 + out_count]
    for lag_index in range(1, short_len):
        begin_row = short_len - 1 - lag_index
        running = running + short_taps[lag_index] * stream[:, begin_row: begin_row + out_count]
    return running


def toeplitz_rows(filters):
    group_count, filter_len = filters.shape
    padded = jnp.concatenate([jnp.zeros((group_count, 1), jnp.float32), filters[:, ::-1], jnp.zeros((group_count, filter_len), jnp.float32)], axis=1)
    tiled = jnp.tile(padded, (1, filter_len))[:, : 2 * filter_len * filter_len]
    return tiled.reshape(group_count, filter_len, 2 * filter_len)


def strand_block(onehot, nuc_block, short_taps, filters):
    filter_len = filters.shape[1]
    short_len = short_taps.shape[1]
    strands = onehot.shape[0]
    out_rows = onehot.shape[1] - (filter_len - 1) - (short_len - 1)
    channel_count = nuc_block.shape[2]
    group_count = filters.shape[0]
    lookup = jnp.einsum("sen,mnc->msec", onehot.astype(jnp.float32), nuc_block.astype(jnp.float32))
    query_rows = causal_taps(lookup[0, :, filter_len - 1:], short_taps[0])
    key_rows = causal_taps(lookup[1], short_taps[1])
    value_rows = causal_taps(lookup[2], short_taps[2])
    key_value = key_rows * value_rows
    padded = jnp.concatenate([jnp.zeros((strands, 1, channel_count), jnp.float32), key_value], axis=1)
    blocks = padded.reshape(strands, out_rows // filter_len + 1, filter_len, group_count, channel_count // group_count)
    paired = jnp.concatenate([blocks[:, :-1], blocks[:, 1:]], axis=2)
    matrix = toeplitz_rows(filters)
    mixed_rows = jnp.einsum("gij,snjgc->snigc", matrix, paired, precision=lax.Precision.HIGHEST)
    mixed_rows = mixed_rows.reshape(strands, out_rows, channel_count)
    return (query_rows * mixed_rows).astype(jnp.bfloat16)


def reference(tokens, nuc_table, short_filter, mr_filter, head_weight):
    filter_len = mr_filter.shape[1]
    short_len = short_filter.shape[1]
    rim_rows = filter_len - 1 + short_len - 1
    seq_length = tokens.shape[0]
    alphabet = jnp.arange(4, dtype=jnp.int32)
    strands = jnp.stack([tokens, 3 - tokens[::-1]])
    onehot = (strands[:, :, None] == alphabet).astype(jnp.float32)
    onehot = jnp.concatenate([jnp.zeros((2, rim_rows, 4), jnp.float32), onehot], axis=1)
    block_width = 256 if D % 256 == 0 else D
    block_count = D // block_width
    nuc_blocks = nuc_table.reshape(3, 4, block_count, block_width).transpose(2, 0, 1, 3)
    tap_blocks = short_filter.reshape(3, short_len, block_count, block_width).transpose(2, 0, 1, 3)
    mr_blocks = mr_filter.reshape(block_count, block_width // GROUP, filter_len)
    head_blocks = head_weight.reshape(TAPS_HEAD, block_count, block_width, HEAD_OUT).transpose(1, 0, 2, 3)
    head_rim = (TAPS_HEAD - 1) // 2

    def add_block(running, block_args):
        nuc_block, short_taps, filters, weight = block_args
        strand_track = strand_block(onehot, nuc_block, short_taps, filters)
        forward_pad = jnp.pad(strand_track[0], ((head_rim, head_rim), (0, 0)))
        reverse_pad = jnp.pad(strand_track[1][::-1], ((head_rim, head_rim), (0, 0)))
        for tap_index in range(TAPS_HEAD):
            mirror_row = TAPS_HEAD - 1 - tap_index
            running = running + jnp.dot(forward_pad[tap_index: tap_index + seq_length], weight[tap_index], preferred_element_type=jnp.float32)
            running = running + jnp.dot(reverse_pad[mirror_row: mirror_row + seq_length], weight[tap_index], preferred_element_type=jnp.float32)
        return running, None

    running, _ = lax.scan(add_block, jnp.zeros((seq_length, HEAD_OUT), jnp.float32), (nuc_blocks, tap_blocks, mr_blocks, head_blocks))
    return running.astype(jnp.bfloat16)
```

```python
import functools

import jax
import jax.numpy as jnp
from jax import lax
from jax.experimental import pallas as pl
from jax.experimental.pallas import tpu as pltpu
from jax.sharding import PartitionSpec as P

LANES = 128
HALF = 64
LETTERS = 4
STRANDS = 2
PARTS = 2
WINDOWS = STRANDS * PARTS
F32 = jnp.float32
BF16 = jnp.bfloat16


def up(value, step):
    return -(-value // step) * step


def iota(shape, dim):
    return lax.broadcasted_iota(jnp.int32, shape, dim)


def dot(a, b):
    return jnp.dot(a, b, preferred_element_type=F32)


def flip_matrix(size):
    return (iota((size, size), 0) + iota((size, size), 1) == size - 1).astype(F32).astype(BF16)


def build_onehot(tok_ref, oh_ref, short_len, window, seg_rows, query_shift, query_rows):
    tok = tok_ref[...]
    width = tok.shape[1]

    def shifted(amount, count):
        return pltpu.roll(tok, (width - amount) % width, 1)[:, :count]

    lags = []
    for lag in range(short_len):
        lead = short_len - lag
        lags.append(
            jnp.concatenate(
                [
                    shifted(lead, window),
                    shifted(lead - 1, LANES),
                    shifted(lead + query_shift, query_rows),
                ],
                axis=1,
            )
        )
    own = lags[0] > 0
    zero = jnp.zeros_like(lags[0])
    lags = [jnp.where(own, lag, zero) for lag in lags]
    while len(lags) % 2:
        lags.append(zero)
    total = lags[0].shape[1]
    row = iota((2 * LETTERS, total), 0)
    first = row < LETTERS
    letter = jnp.where(first, row, row - LETTERS) + 1
    blocks = []
    for x in range(WINDOWS):
        pieces = []
        for pair in range(len(lags) // 2):
            a = jnp.broadcast_to(lags[2 * pair][x : x + 1], (2 * LETTERS, total))
            b = jnp.broadcast_to(lags[2 * pair + 1][x : x + 1], (2 * LETTERS, total))
            pieces.append((jnp.where(first, a, b) == letter).astype(F32))
        blocks += pieces + pieces
    oh_ref[...] = jnp.concatenate(blocks, axis=0).T.astype(BF16)


def build_weights(nuc_ref, sf_ref, wn_ref, short_len):
    row = iota((2 * LETTERS, LANES), 0)
    first = row < LETTERS
    pairs = (short_len + 1) // 2

    def step(v, carry):
        lanes = pl.ds(pl.multiple_of(v * LANES, LANES), LANES)
        for m in range(3):
            nuc = nuc_ref[m, :, lanes].astype(F32)
            nuc = jnp.concatenate([nuc, nuc], axis=0)
            taps = sf_ref[m, :, lanes]
            pieces = []
            for pair in range(pairs):
                a = jnp.broadcast_to(taps[2 * pair : 2 * pair + 1], row.shape)
                if 2 * pair + 1 < short_len:
                    b = jnp.broadcast_to(taps[2 * pair + 1 : 2 * pair + 2], row.shape)
                else:
                    b = jnp.zeros(row.shape, F32)
                pieces.append(jnp.where(first, a, b) * nuc)
            product = jnp.concatenate(pieces, axis=0)
            high = product.astype(BF16).astype(F32)
            full = jnp.concatenate([high, product - high], axis=0)
            turned = pltpu.roll(full, HALF, 1)
            low_half = iota(full.shape, 1) < HALF
            zero = jnp.zeros_like(full)
            wn_ref[m, 0, :, lanes] = jnp.where(low_half, full, zero).astype(BF16)
            wn_ref[m, 1, :, lanes] = jnp.where(low_half, zero, turned).astype(BF16)
            wn_ref[m, 2, :, lanes] = jnp.where(low_half, zero, full).astype(BF16)
            wn_ref[m, 3, :, lanes] = jnp.where(low_half, turned, zero).astype(BF16)
        return carry

    lax.fori_loop(0, nuc_ref.shape[2] // LANES, step, 0)


def toeplitz(reverse_row, rows):
    taps = reverse_row.shape[1]
    turned = pltpu.roll(jnp.broadcast_to(reverse_row, (taps, taps)), 0, 1, stride=1, stride_axis=0)
    turned = jnp.concatenate([turned, turned[: rows - taps]], axis=0)
    gap = iota((rows, taps), 0) - iota((rows, taps), 1)
    zero = jnp.zeros_like(turned)
    near = jnp.where((gap <= 1) & (gap >= 2 - taps), turned, zero)
    far = jnp.where(gap >= 2, turned, zero)
    return jnp.concatenate([near, far], axis=1).astype(BF16)


def kernel(
    sizes, tok_ref, nuc_ref, sf_ref, mr_ref, hw_hbm, out_ref,
    oh_ref, wn_ref, fr_ref, track_ref, hw_ref, ps_ref, sem,
):
    rows, short_len, taps, group_width, head_taps = sizes
    channels = nuc_ref.shape[2]
    window = 2 * taps
    part_rows = (rows + head_taps - 1) // PARTS
    track_rows = up(part_rows, 16)
    query_shift = taps - 2
    query_rows = up(track_rows, LANES)

    fetch = pltpu.make_async_copy(hw_hbm, hw_ref, sem)
    fetch.start()

    build_onehot(tok_ref, oh_ref, short_len, window, LANES, query_shift, query_rows)
    build_weights(nuc_ref, sf_ref, wn_ref, short_len)
    place = iota((taps, taps), 0) + iota((taps, taps), 1)
    turn = (place == taps - 2) | (place == 2 * taps - 2)
    fr_ref[...] = dot(mr_ref[...].astype(BF16), turn.astype(F32).astype(BF16))

    groups_in_half = HALF // group_width
    lane_group = (iota((track_rows, 2 * LANES), 1) % HALF) // group_width
    fix_group = lane_group[:8]
    fix_row = iota((8, 2 * LANES), 0) == 0

    def step(v, carry):
        lanes = pl.ds(pl.multiple_of(v * LANES, LANES), LANES)
        per_step = LANES // group_width
        taps_rev = fr_ref[pl.ds(pl.multiple_of(v * per_step, per_step), per_step), :]
        kv_hot = oh_ref[: window + 16, :]
        q_hot = oh_ref[window + LANES : window + LANES + track_rows, :]
        products = []
        for half in range(2):
            def weights(m):
                a = wn_ref[m, 2 * half, :, lanes]
                b = wn_ref[m, 2 * half + 1, :, lanes]
                z = jnp.zeros_like(a)
                left = jnp.concatenate([a, b, z, z], axis=0)
                right = jnp.concatenate([z, z, a, b], axis=0)
                return jnp.concatenate([left, right], axis=1)

            gated = dot(kv_hot, weights(1)) * dot(kv_hot, weights(2))
            query = dot(q_hot, weights(0))
            data = gated[:window].astype(BF16)
            before = jnp.broadcast_to(gated[window : window + 1], fix_row.shape)
            mixed = None
            fix = None
            for g in range(groups_in_half):
                index = half * groups_in_half + g
                taps_row = taps_rev[index : index + 1]
                piece = dot(toeplitz(taps_row, track_rows), data)
                last = jnp.broadcast_to(taps_row[:, taps - 1 :], fix_row.shape)
                mixed = piece if g == 0 else jnp.where(lane_group == g, piece, mixed)
                fix = last if g == 0 else jnp.where(fix_group == g, last, fix)
            fix = jnp.where(fix_row, fix * before, 0.0)
            mixed = jnp.concatenate([mixed[:8] + fix, mixed[8:]], axis=0)
            products.append(query * mixed)
        low_half = iota((track_rows, LANES), 1) < HALF
        for n in range(2):
            a = products[0][:, n * LANES : (n + 1) * LANES]
            b = products[1][:, n * LANES : (n + 1) * LANES]
            even = jnp.where(low_half, a, b)
            odd = pltpu.roll(jnp.where(low_half, b, a), HALF, 1)
            at = 2 * n * track_rows
            track_ref[at : at + track_rows, lanes] = even.astype(BF16)
            track_ref[at + track_rows : at + 2 * track_rows, lanes] = odd.astype(BF16)
        return carry

    lax.fori_loop(0, channels // LANES, step, 0)

    fetch.wait()
    totals = [None, None]
    for k in range(head_taps):
        score = dot(track_ref[...], hw_ref[k])
        for s in range(STRANDS):
            at = 2 * s * track_rows
            ps_ref[s, :track_rows] = score[at : at + track_rows]
            ps_ref[s, part_rows : part_rows + track_rows] = score[at + track_rows : at + 2 * track_rows]
            part = ps_ref[s, k : k + rows]
            totals[s] = part if k == 0 else totals[s] + part
    forward, backward = totals
    flip = flip_matrix(rows)
    for _ in range(3):
        high = backward.astype(BF16)
        forward = forward + dot(flip, high)
        backward = backward - high.astype(F32)
    out_ref[...] = forward


def shards(tokens, nuc_table, short_filter, mr_filter, head_weight):
    rows = tokens.shape[0]
    _, short_len, channels = short_filter.shape
    filters, taps = mr_filter.shape
    head_taps, _, outs = head_weight.shape
    rim = (head_taps - 1) // 2
    reach = taps - 1 + short_len - 1 + rim
    part_rows = (rows + 2 * rim) // PARTS
    window = 2 * taps
    width = up(window + short_len, LANES)
    count = lax.axis_size("seq")

    coded = tokens + 1
    before = lax.ppermute(coded[rows - reach :], "seq", [(i, i + 1) for i in range(count - 1)])
    after = lax.ppermute(coded[:reach], "seq", [(i + 1, i) for i in range(count - 1)])
    forward = jnp.concatenate([before, coded, after])
    backward = jnp.where(forward > 0, LETTERS + 1 - forward, 0)[::-1]
    lanes = []
    for strand in (forward, backward):
        for n in range(PARTS):
            lanes.append(strand[n * part_rows : n * part_rows + width])
    lanes += [jnp.zeros_like(lanes[0])] * (8 - WINDOWS)
    letters = jnp.stack(lanes)

    track_rows = up(part_rows, 16)
    hot_rows = window + LANES + up(track_rows, LANES)
    hot_depth = WINDOWS * 2 * LETTERS * up(short_len, 2)
    vmem = pl.BlockSpec(memory_space=pltpu.VMEM)
    partial = pl.pallas_call(
        functools.partial(kernel, (rows, short_len, taps, channels // filters, head_taps)),
        out_shape=jax.ShapeDtypeStruct((rows, outs), F32),
        in_specs=[vmem, vmem, vmem, vmem, pl.BlockSpec(memory_space=pl.ANY)],
        out_specs=vmem,
        scratch_shapes=[
            pltpu.VMEM((hot_rows, hot_depth), BF16),
            pltpu.VMEM((3, 4, hot_depth // WINDOWS, channels), BF16),
            pltpu.VMEM((filters, taps), F32),
            pltpu.VMEM((WINDOWS * track_rows, channels), BF16),
            pltpu.VMEM(head_weight.shape, BF16),
            pltpu.VMEM((STRANDS, part_rows + track_rows + 6, outs), F32),
            pltpu.SemaphoreType.DMA,
        ],
        compiler_params=pltpu.CompilerParams(vmem_limit_bytes=40 * 1024 * 1024),
        cost_estimate=pl.CostEstimate(
            flops=2 * 4 * 10**9, bytes_accessed=8 * 10**6, transcendentals=0
        ),
    )(letters, nuc_table, short_filter, mr_filter, head_weight)

    cores = lax.axis_size("ch")
    ring = [(i, (i + 1) % cores) for i in range(cores)]
    total, moving = partial, partial
    for _ in range(cores - 1):
        moving = lax.ppermute(moving, "ch", ring)
        total = total + moving
    return total.astype(BF16)


def solution(mesh):
    in_specs = (
        P(("groups", "seq")),
        P(None, None, "ch"),
        P(None, None, "ch"),
        P("ch", None),
        P(None, "ch", None),
    )
    out_specs = P(("groups", "seq"), None)
    return jax.shard_map(shards, mesh=mesh, in_specs=in_specs, out_specs=out_specs, check_vma=False)
```

```python
import functools

import jax
import jax.numpy as jnp
from jax import lax
from jax.experimental import pallas as pl
from jax.experimental.pallas import tpu as pltpu
from jax.sharding import PartitionSpec as P

LANES = 128
HALF = 64
WIDE = 256
LETTERS = 4
STRANDS = 2
PARTS = 2
WINDOWS = STRANDS * PARTS
F32 = jnp.float32
BF16 = jnp.bfloat16


def up(value, step):
    return -(-value // step) * step


def iota(shape, dim):
    return lax.broadcasted_iota(jnp.int32, shape, dim)


def dot(a, b):
    return jnp.dot(a, b, preferred_element_type=F32)


def flip_matrix(size):
    return (iota((size, size), 0) + iota((size, size), 1) == size - 1).astype(F32).astype(BF16)


def build_onehot(tok_ref, hot_ref, query_ref, short_len, window, query_shift):
    tok = tok_ref[...]
    width = tok.shape[1]
    hot_rows = hot_ref.shape[0] // WINDOWS
    query_rows = query_ref.shape[0] // WINDOWS
    query_lanes = up(query_rows, LANES)

    def shifted(amount, count):
        return pltpu.roll(tok, (width - amount) % width, 1)[:, :count]

    lags = []
    for lag in range(short_len):
        lead = short_len - lag
        lags.append(
            jnp.concatenate(
                [
                    shifted(lead, window),
                    shifted(lead - 1, LANES),
                    shifted(lead + query_shift, query_lanes),
                ],
                axis=1,
            )
        )
    own = lags[0] > 0
    zero = jnp.zeros_like(lags[0])
    lags = [jnp.where(own, lag, zero) for lag in lags]
    while len(lags) % 2:
        lags.append(zero)
    total = lags[0].shape[1]
    row = iota((2 * LETTERS, total), 0)
    first = row < LETTERS
    letter = jnp.where(first, row, row - LETTERS) + 1
    for x in range(WINDOWS):
        pieces = []
        for pair in range(len(lags) // 2):
            a = jnp.broadcast_to(lags[2 * pair][x : x + 1], (2 * LETTERS, total))
            b = jnp.broadcast_to(lags[2 * pair + 1][x : x + 1], (2 * LETTERS, total))
            pieces.append((jnp.where(first, a, b) == letter).astype(F32))
        hot = jnp.concatenate(pieces + pieces, axis=0).T.astype(BF16)
        hot_ref[x * hot_rows : (x + 1) * hot_rows] = hot[:hot_rows]
        at = window + LANES
        query_ref[x * query_rows : (x + 1) * query_rows] = hot[at : at + query_rows]


def build_weights(nuc_ref, sf_ref, wn_ref, short_len):
    row = iota((2 * LETTERS, WIDE), 0)
    first = row < LETTERS
    pairs = (short_len + 1) // 2

    def step(v, carry):
        lanes = pl.ds(pl.multiple_of(v * WIDE, WIDE), WIDE)
        for m in range(3):
            nuc = nuc_ref[m, :, lanes].astype(F32)
            nuc = jnp.concatenate([nuc, nuc], axis=0)
            taps = sf_ref[m, :, lanes]
            pieces = []
            for pair in range(pairs):
                a = jnp.broadcast_to(taps[2 * pair : 2 * pair + 1], row.shape)
                if 2 * pair + 1 < short_len:
                    b = jnp.broadcast_to(taps[2 * pair + 1 : 2 * pair + 2], row.shape)
                else:
                    b = jnp.zeros(row.shape, F32)
                pieces.append(jnp.where(first, a, b) * nuc)
            product = jnp.concatenate(pieces, axis=0)
            high = product.astype(BF16)
            low = (product - high.astype(F32)).astype(BF16)
            wn_ref[m, :, lanes] = jnp.concatenate([high, low], axis=0)
        return carry

    lax.fori_loop(0, nuc_ref.shape[2] // WIDE, step, 0)


def toeplitz(reverse_row, rows):
    taps = reverse_row.shape[1]
    turned = pltpu.roll(jnp.broadcast_to(reverse_row, (taps, taps)), 0, 1, stride=1, stride_axis=0)
    turned = jnp.concatenate([turned, turned[: rows - taps]], axis=0)
    gap = iota((rows, taps), 0) - iota((rows, taps), 1)
    zero = jnp.zeros_like(turned)
    near = jnp.where((gap <= 1) & (gap >= 2 - taps), turned, zero)
    far = jnp.where(gap >= 2, turned, zero)
    return jnp.concatenate([near, far], axis=1).astype(BF16)


def kernel(
    sizes, tok_ref, nuc_hbm, sf_hbm, mr_hbm, hw_hbm, out_ref,
    nuc_ref, sf_ref, mr_ref, hw_ref, hot_ref, query_ref, wn_ref, fr_ref, track_ref, ps_ref, sems,
):
    rows, short_len, taps, group_width, head_taps = sizes
    channels = nuc_ref.shape[2]
    window = 2 * taps
    part_rows = (rows + head_taps - 1) // PARTS
    track_rows = up(part_rows, 16)
    used_rows = window + 8
    hot_rows = window + 16

    pairs = [(nuc_hbm, nuc_ref), (sf_hbm, sf_ref), (mr_hbm, mr_ref), (hw_hbm, hw_ref)]
    copies = [pltpu.make_async_copy(a, b, sems.at[i]) for i, (a, b) in enumerate(pairs)]
    for copy in copies:
        copy.start()
    fetch = copies[-1]

    build_onehot(tok_ref, hot_ref, query_ref, short_len, window, taps - 2)
    for copy in copies[:-1]:
        copy.wait()
    build_weights(nuc_ref, sf_ref, wn_ref, short_len)
    place = iota((taps, taps), 0) + iota((taps, taps), 1)
    turn = (place == taps - 2) | (place == 2 * taps - 2)
    fr_ref[...] = dot(mr_ref[...].astype(BF16), turn.astype(F32).astype(BF16))

    tile_groups = HALF // group_width
    lane_group = (iota((track_rows, WIDE), 1) % HALF) // group_width
    fix_group = lane_group[:8]
    fix_row = iota((8, WIDE), 0) == 0

    def mix(taps_rows, merged):
        data = merged[:window].astype(BF16)
        before = jnp.broadcast_to(merged[window : window + 1], fix_row.shape)
        mixed = None
        fix = None
        for g in range(tile_groups):
            taps_row = taps_rows[g : g + 1]
            piece = dot(toeplitz(taps_row, track_rows), data)
            last = jnp.broadcast_to(taps_row[:, taps - 1 :], fix_row.shape)
            mixed = piece if g == 0 else jnp.where(lane_group == g, piece, mixed)
            fix = last if g == 0 else jnp.where(fix_group == g, last, fix)
        fix = jnp.where(fix_row, fix * before, 0.0)
        return jnp.concatenate([mixed[:8] + fix, mixed[8:]], axis=0)

    def step(v, carry):
        lanes = pl.ds(pl.multiple_of(v * WIDE, WIDE), WIDE)
        per_step = WIDE // group_width
        taps_rev = fr_ref[pl.ds(pl.multiple_of(v * per_step, per_step), per_step), :]
        hot = hot_ref[...]
        gated = dot(hot, wn_ref[1, :, lanes]) * dot(hot, wn_ref[2, :, lanes])
        query = dot(query_ref[...], wn_ref[0, :, lanes])
        low_half = iota((used_rows, LANES), 1) < HALF
        low_track = low_half[:track_rows]
        for j in range(2):
            column = gated[:, j * LANES : (j + 1) * LANES]
            part = [column[x * hot_rows : x * hot_rows + used_rows] for x in range(WINDOWS)]
            lower, upper = [], []
            for x in range(0, WINDOWS, 2):
                turned = pltpu.roll(part[x + 1], HALF, 1)
                lower.append(jnp.where(low_half, part[x], turned))
                upper.append(jnp.where(low_half, turned, part[x]))
            at = 2 * j * tile_groups
            lower = mix(taps_rev[at : at + tile_groups], jnp.concatenate(lower, axis=1))
            upper = mix(taps_rev[at + tile_groups : at + 2 * tile_groups], jnp.concatenate(upper, axis=1))
            to = pl.ds(pl.multiple_of(v * WIDE + j * LANES, LANES), LANES)
            for x in range(0, WINDOWS, 2):
                a = lower[:, x * HALF : x * HALF + LANES]
                b = upper[:, x * HALF : x * HALF + LANES]
                even = jnp.where(low_track, a, b)
                odd = pltpu.roll(jnp.where(low_track, b, a), HALF, 1)
                for y, mixed in ((x, even), (x + 1, odd)):
                    at = y * track_rows
                    own = query[at : at + track_rows, j * LANES : (j + 1) * LANES]
                    track_ref[at : at + track_rows, to] = (own * mixed).astype(BF16)
        return carry

    lax.fori_loop(0, channels // WIDE, step, 0)

    fetch.wait()
    totals = [None, None]
    for k in range(head_taps):
        score = dot(track_ref[...], hw_ref[k])
        for s in range(STRANDS):
            at = 2 * s * track_rows
            ps_ref[s, :track_rows] = score[at : at + track_rows]
            ps_ref[s, part_rows : part_rows + track_rows] = score[at + track_rows : at + 2 * track_rows]
            part = ps_ref[s, k : k + rows]
            totals[s] = part if k == 0 else totals[s] + part
    forward, backward = totals
    flip = flip_matrix(rows)
    for _ in range(3):
        high = backward.astype(BF16)
        forward = forward + dot(flip, high)
        backward = backward - high.astype(F32)
    out_ref[...] = forward


def neighbour_ways(count, cores):
    ways = []
    for i in range(count):
        for c in range(cores):
            step = 1 if (i + c) % 2 == 0 else -1
            there = (i + step, c ^ 1) if 0 <= i + step < count else (i, c ^ 1)
            ways.append((i * cores + c, there[0] * cores + there[1]))
    return ways


def shards(tokens, nuc_table, short_filter, mr_filter, head_weight):
    rows = tokens.shape[0]
    _, short_len, channels = short_filter.shape
    filters, taps = mr_filter.shape
    head_taps, _, outs = head_weight.shape
    rim = (head_taps - 1) // 2
    reach = taps - 1 + short_len - 1 + rim
    part_rows = (rows + 2 * rim) // PARTS
    window = 2 * taps
    width = up(window + short_len, LANES)
    count = lax.axis_size("seq")

    cores = lax.axis_size("ch")
    place = lax.axis_index("seq")
    ways = neighbour_ways(count, cores)
    one = lax.ppermute(tokens, ("seq", "ch"), ways)
    two = lax.ppermute(tokens, ("seq", "ch"), [(b, a) for a, b in ways])
    onward = (place + lax.axis_index("ch")) % 2 == 0
    before = jnp.where(onward, one, two)[rows - reach :]
    after = jnp.where(onward, two, one)[:reach]
    forward = jnp.concatenate([before, tokens, after])
    position = place * rows - reach + jnp.arange(forward.shape[0], dtype=jnp.int32)
    inside = (position >= 0) & (position < count * rows)
    backward = jnp.where(inside, LETTERS - forward, 0)[::-1]
    forward = jnp.where(inside, forward + 1, 0)
    lanes = []
    for strand in (forward, backward):
        for n in range(PARTS):
            lanes.append(strand[n * part_rows : n * part_rows + width])
    lanes += [jnp.zeros_like(lanes[0])] * (8 - WINDOWS)
    letters = jnp.stack(lanes)

    track_rows = up(part_rows, 16)
    hot_depth = 2 * LETTERS * up(short_len, 2)
    vmem = pl.BlockSpec(memory_space=pltpu.VMEM)
    hbm = pl.BlockSpec(memory_space=pltpu.HBM)
    partial = pl.pallas_call(
        functools.partial(kernel, (rows, short_len, taps, channels // filters, head_taps)),
        out_shape=jax.ShapeDtypeStruct((rows, outs), F32),
        in_specs=[vmem, hbm, hbm, hbm, hbm],
        out_specs=vmem,
        scratch_shapes=[
            pltpu.VMEM(nuc_table.shape, BF16),
            pltpu.VMEM(short_filter.shape, F32),
            pltpu.VMEM(mr_filter.shape, F32),
            pltpu.VMEM(head_weight.shape, BF16),
            pltpu.VMEM((WINDOWS * (window + 16), hot_depth), BF16),
            pltpu.VMEM((WINDOWS * track_rows, hot_depth), BF16),
            pltpu.VMEM((3, hot_depth, channels), BF16),
            pltpu.VMEM((filters, taps), F32),
            pltpu.VMEM((WINDOWS * track_rows, channels), BF16),
            pltpu.VMEM((STRANDS, part_rows + track_rows + 6, outs), F32),
            pltpu.SemaphoreType.DMA((4,)),
        ],
        compiler_params=pltpu.CompilerParams(vmem_limit_bytes=63 * 1024 * 1024),
        cost_estimate=pl.CostEstimate(
            flops=2 * 4 * 10**9, bytes_accessed=8 * 10**6, transcendentals=0
        ),
    )(letters, nuc_table, short_filter, mr_filter, head_weight)

    ring = [(i, (i + 1) % cores) for i in range(cores)]
    total, moving = partial, partial
    for _ in range(cores - 1):
        moving = lax.ppermute(moving, "ch", ring)
        total = total + moving
    return total.astype(BF16)


def solution(mesh):
    in_specs = (
        P(("groups", "seq")),
        P(None, None, "ch"),
        P(None, None, "ch"),
        P("ch", None),
        P(None, "ch", None),
    )
    out_specs = P(("groups", "seq"), None)
    return jax.shard_map(shards, mesh=mesh, in_specs=in_specs, out_specs=out_specs, check_vma=False)
```

```python
import functools

import jax
import jax.numpy as jnp
from jax import lax
from jax.experimental import pallas as pl
from jax.experimental.pallas import tpu as pltpu
from jax.sharding import PartitionSpec as P

LANES = 128
HALF = 64
WIDE = 256
SUB = 8
PACK = 16
LETTERS = 4
STRANDS = 2
PARTS = 2
F32 = jnp.float32
BF16 = jnp.bfloat16
MIB = 1024 * 1024


def up(value, step):
    return -(-value // step) * step


def iota(shape, dim):
    return lax.broadcasted_iota(jnp.int32, shape, dim)


def dot(a, b):
    return jnp.dot(a, b, preferred_element_type=F32)


def ones_where(mask):
    return mask.astype(F32).astype(BF16)


class Plan:
    def __init__(self, rows, short_len, taps, head_taps):
        self.rows, self.short_len, self.taps, self.head_taps = rows, short_len, taps, head_taps
        self.rim = (head_taps - 1) // 2
        self.part = rows // PARTS
        self.window = 2 * taps
        self.offset = self.window - self.part - 2 * self.rim
        self.missing = taps - 1 - self.offset
        self.mix_rows = up(self.part + 2 * self.rim, PACK)
        self.track_rows = (PARTS - 1) * self.part + self.mix_rows
        self.hot_rows = PACK + (PARTS - 1) * self.part + self.window
        self.lead = PACK + self.offset + self.rim + short_len - 1
        self.query_lead = PACK + self.offset
        self.width = up(self.query_lead + self.track_rows + short_len, LANES)
        self.depth = 2 * LETTERS * up(short_len, 2)


def build_weights(plan, nuc_ref, sf_ref, wn_ref):
    row = iota((2 * LETTERS, WIDE), 0)
    first = row < LETTERS
    short_len = plan.short_len

    def step(v, carry):
        lanes = pl.ds(pl.multiple_of(v * WIDE, WIDE), WIDE)
        for m in range(3):
            nuc = nuc_ref[m, :, lanes].astype(F32)
            nuc = jnp.concatenate([nuc, nuc], axis=0)
            taps = sf_ref[m, :, lanes]
            pieces = []
            for lag in range(0, short_len, 2):
                a = jnp.broadcast_to(taps[lag : lag + 1], row.shape)
                if lag + 1 < short_len:
                    b = jnp.broadcast_to(taps[lag + 1 : lag + 2], row.shape)
                else:
                    b = jnp.zeros(row.shape, F32)
                pieces.append(jnp.where(first, a, b) * nuc)
            product = jnp.concatenate(pieces, axis=0)
            high = product.astype(BF16)
            low = (product - high.astype(F32)).astype(BF16)
            wn_ref[m, :, lanes] = jnp.concatenate([high, low], axis=0)
        return carry

    lax.fori_loop(0, nuc_ref.shape[2] // WIDE, step, 0)


def build_mixers(plan, mr_ref, fr_ref, mixer_ref):
    taps, rows = plan.taps, plan.mix_rows
    total = iota((taps, taps), 0) + iota((taps, taps), 1)
    turn = (total == plan.offset) | (total == plan.offset + taps)
    fr_ref[...] = dot(mr_ref[...].astype(BF16), ones_where(turn))
    gap = iota((rows, taps), 0) - iota((rows, taps), 1)
    near_mask = (gap <= plan.missing) & (gap >= -plan.offset)
    far_mask = gap > plan.missing
    filters = mr_ref.shape[0]

    def step(b, carry):
        block = fr_ref[pl.ds(pl.multiple_of(b * SUB, SUB), SUB), :]
        for g in range(SUB):
            wide = jnp.broadcast_to(block[g : g + 1], (taps, taps))
            turned = pltpu.roll(wide, 0, 1, stride=1, stride_axis=0)
            turned = jnp.concatenate([turned, turned[: rows - taps]], axis=0)
            zero = jnp.zeros_like(turned)
            at = pl.ds(pl.multiple_of((b * SUB + g) * rows, rows), rows)
            mixer_ref[at, :taps] = jnp.where(near_mask, turned, zero).astype(BF16)
            mixer_ref[at, taps:] = jnp.where(far_mask, turned, zero).astype(BF16)
        return carry

    lax.fori_loop(0, filters // SUB, step, 0)


def build_edges(plan, mr_ref, edge_ref):
    filters, taps = mr_ref.shape
    channels = edge_ref.shape[1]
    rows = edge_ref.shape[0]
    row, tap = iota((rows, taps), 0), iota((rows, taps), 1)
    wanted = tap == row % SUB + plan.offset + 1 + row // SUB
    picked = lax.dot_general(
        ones_where(wanted), mr_ref[...].astype(BF16), (((1,), (1,)), ((), ())), preferred_element_type=F32
    ).astype(BF16)
    width = channels // filters

    def step(v, carry):
        shape = (filters, WIDE)
        spread = ones_where(iota(shape, 0) == (iota(shape, 1) + v * WIDE) // width)
        edge_ref[:, pl.ds(pl.multiple_of(v * WIDE, WIDE), WIDE)] = dot(picked, spread)
        return carry

    lax.fori_loop(0, channels // WIDE, step, 0)


def prepare(
    plan, own_hbm, nuc_hbm, sf_hbm, mr_hbm, own_ref, wn_ref, mixer_ref, edge_ref,
    nuc_ref, sf_ref, mr_ref, fr_ref, sems,
):
    pairs = [(mr_hbm, mr_ref), (nuc_hbm, nuc_ref), (sf_hbm, sf_ref), (own_hbm, own_ref)]
    copies = [pltpu.make_async_copy(a, b, sems.at[i]) for i, (a, b) in enumerate(pairs)]
    for copy in copies:
        copy.start()
    copies[0].wait()
    build_mixers(plan, mr_ref, fr_ref, mixer_ref)
    build_edges(plan, mr_ref, edge_ref)
    for copy in copies[1:]:
        copy.wait()
    build_weights(plan, nuc_ref, sf_ref, wn_ref)


def coded_letters(plan, count, one_ref, own_ref, two_ref):
    place = lax.axis_index("seq")
    onward = lax.rem(place + lax.axis_index("ch"), 2) == 0
    one, two = one_ref[...], two_ref[...]
    before = jnp.where(onward, one, two) + 1
    after = jnp.where(onward, two, one) + 1
    before = jnp.where(place > 0, before, 0)
    after = jnp.where(place < count - 1, after, 0)
    around = jnp.concatenate([before, own_ref[...] + 1, after], axis=1)
    blocks = around.shape[1] // LANES
    pieces = [around[:, i * LANES : (i + 1) * LANES] for i in range(blocks)]
    pieces += [jnp.zeros_like(pieces[0])] * (up(blocks, SUB) - blocks)
    flip = ones_where(iota((LANES, LANES), 0) + iota((LANES, LANES), 1) == LANES - 1)
    turned = dot(jnp.concatenate(pieces, axis=0).astype(F32).astype(BF16), flip).astype(jnp.int32)
    back = jnp.concatenate([turned[i : i + 1] for i in reversed(range(blocks))], axis=1)
    back = jnp.where(back > 0, LETTERS + 1 - back, 0)
    rest = jnp.zeros((SUB - STRANDS, around.shape[1]), jnp.int32)
    return jnp.concatenate([around, back, rest], axis=0)


def build_onehot(plan, tok, hot_ref, query_ref):
    width = tok.shape[1]
    hot_lanes, query_lanes = up(plan.hot_rows, LANES), up(plan.track_rows, LANES)
    lags = []
    for lag in range(plan.short_len):
        lead = plan.rows - plan.lead + plan.short_len - 1 - lag
        a = pltpu.roll(tok, (width - lead) % width, 1)[:, :hot_lanes]
        b = pltpu.roll(tok, (width - lead - plan.query_lead) % width, 1)[:, :query_lanes]
        lags.append(jnp.concatenate([a, b], axis=1))
    own = lags[0] > 0
    zero = jnp.zeros_like(lags[0])
    lags = [jnp.where(own, lag, zero) for lag in lags]
    if len(lags) % 2:
        lags.append(zero)
    row = iota((2 * LETTERS, zero.shape[1]), 0)
    first = row < LETTERS
    letter = jnp.where(first, row, row - LETTERS) + 1
    for s in range(STRANDS):
        pieces = []
        for lag in range(0, len(lags), 2):
            a = jnp.broadcast_to(lags[lag][s : s + 1], row.shape)
            b = jnp.broadcast_to(lags[lag + 1][s : s + 1], row.shape)
            pieces.append((jnp.where(first, a, b) == letter).astype(F32))
        hot = jnp.concatenate(pieces + pieces, axis=0).T.astype(BF16)
        hot_ref[s] = hot[: plan.hot_rows]
        query_ref[s] = hot[hot_lanes : hot_lanes + plan.track_rows]


def kernel(
    plan, count, one_ref, own_ref, two_ref, wn_ref, mixer_ref, edge_ref, hw_hbm, out_ref,
    hw_ref, hot_ref, query_ref, track_ref, score_ref, sem,
):
    channels = wn_ref.shape[2]
    part, window, mix_rows = plan.part, plan.window, plan.mix_rows
    group_width = channels * mix_rows // mixer_ref.shape[0]
    tile_groups = HALF // group_width
    tile_rows = tile_groups * mix_rows

    fetch = pltpu.make_async_copy(hw_hbm, hw_ref, sem)
    fetch.start()
    tok = coded_letters(plan, count, one_ref, own_ref, two_ref)
    build_onehot(plan, tok, hot_ref, query_ref)

    lane_group = (iota((mix_rows, WIDE), 1) % HALF) // group_width
    low_half = iota((window, LANES), 1) < HALF
    low_mix = low_half[:mix_rows]

    def step(v, carry):
        lanes = pl.ds(pl.multiple_of(v * WIDE, WIDE), WIDE)
        gated, query = [], []
        for s in range(STRANDS):
            gated.append(dot(hot_ref[s], wn_ref[1, :, lanes]) * dot(hot_ref[s], wn_ref[2, :, lanes]))
            query.append(dot(query_ref[s], wn_ref[0, :, lanes]))
        for j in range(WIDE // LANES):
            some = slice(j * LANES, (j + 1) * LANES)
            to = pl.ds(pl.multiple_of(v * WIDE + j * LANES, LANES), LANES)
            lower, upper = [], []
            for s in range(STRANDS):
                a = gated[s][PACK : PACK + window, some]
                b = pltpu.roll(gated[s][PACK + part : PACK + part + window, some], HALF, 1)
                lower.append(jnp.where(low_half, a, b))
                upper.append(jnp.where(low_half, b, a))
            mixed = []
            for h, halves in enumerate((lower, upper)):
                data = jnp.concatenate(halves, axis=1).astype(BF16)
                tile = v * (WIDE // HALF) + 2 * j + h
                mixers = mixer_ref[pl.ds(pl.multiple_of(tile * tile_rows, tile_rows), tile_rows), :]
                pieces = dot(mixers, data)
                chosen = pieces[:mix_rows]
                for g in range(1, tile_groups):
                    chosen = jnp.where(lane_group == g, pieces[g * mix_rows : (g + 1) * mix_rows], chosen)
                mixed.append(chosen)
            for s in range(STRANDS):
                a, b = (m[:, s * LANES : (s + 1) * LANES] for m in mixed)
                both = [jnp.where(low_mix, a, b), pltpu.roll(jnp.where(low_mix, b, a), HALF, 1)]
                for p in range(PARTS):
                    fix = both[p][:SUB]
                    for d in range(plan.missing):
                        at = PACK + p * part - 1 - d
                        fix = fix + edge_ref[d * SUB : (d + 1) * SUB, to] * gated[s][at : at + 1, some]
                    length = part if p < PARTS - 1 else mix_rows
                    whole = jnp.concatenate([fix, both[p][SUB:length]], axis=0)
                    own = query[s][p * part : p * part + length, some]
                    at = s * plan.track_rows + p * part
                    track_ref[at : at + length, to] = (own * whole).astype(BF16)
        return carry

    lax.fori_loop(0, channels // WIDE, step, 0)

    fetch.wait()
    totals = [None, None]
    for k in range(plan.head_taps):
        score = dot(track_ref[...], hw_ref[k])
        for s in range(STRANDS):
            score_ref[s] = score[s * plan.track_rows : (s + 1) * plan.track_rows]
            shifted = score_ref[s, k : k + plan.rows]
            totals[s] = shifted if k == 0 else totals[s] + shifted
    forward, backward = totals
    flip = ones_where(iota((plan.rows, plan.rows), 0) + iota((plan.rows, plan.rows), 1) == plan.rows - 1)
    for _ in range(3):
        high = backward.astype(BF16)
        forward = forward + dot(flip, high)
        backward = backward - high.astype(F32)
    out_ref[...] = forward


def neighbour_ways(count, cores):
    ways = []
    for i in range(count):
        for c in range(cores):
            step = 1 if (i + c) % 2 == 0 else -1
            there = (i + step, c ^ 1) if 0 <= i + step < count else (i, c ^ 1)
            ways.append((i * cores + c, there[0] * cores + there[1]))
    return ways


def stay(array):
    return pltpu.with_memory_space_constraint(array, pltpu.HBM)


def shards(tokens, nuc_table, short_filter, mr_filter, head_weight):
    _, short_len, channels = short_filter.shape
    filters, taps = mr_filter.shape
    head_taps, _, outs = head_weight.shape
    plan = Plan(tokens.shape[0], short_len, taps, head_taps)
    vmem = pl.BlockSpec(memory_space=pltpu.VMEM)
    hbm = pl.BlockSpec(memory_space=pl.ANY)

    own = tokens.reshape(1, plan.rows)
    own_here, weights, mixers, edges = pl.pallas_call(
        functools.partial(prepare, plan),
        out_shape=(
            jax.ShapeDtypeStruct(own.shape, own.dtype),
            jax.ShapeDtypeStruct((3, plan.depth, channels), BF16),
            jax.ShapeDtypeStruct((filters * plan.mix_rows, plan.window), BF16),
            jax.ShapeDtypeStruct((up(plan.missing, 1) * SUB, channels), F32),
        ),
        in_specs=[hbm] * 4,
        out_specs=(vmem,) * 4,
        scratch_shapes=[
            pltpu.VMEM(nuc_table.shape, BF16),
            pltpu.VMEM(short_filter.shape, F32),
            pltpu.VMEM(mr_filter.shape, F32),
            pltpu.VMEM(mr_filter.shape, F32),
            pltpu.SemaphoreType.DMA((4,)),
        ],
        compiler_params=pltpu.CompilerParams(vmem_limit_bytes=16 * MIB),
        cost_estimate=pl.CostEstimate(flops=10**8, bytes_accessed=10**7, transcendentals=0),
        name="prepare",
    )(*(stay(a) for a in (own, nuc_table, short_filter, mr_filter)))

    count, cores = lax.axis_size("seq"), lax.axis_size("ch")
    ways = neighbour_ways(count, cores)
    one = lax.ppermute(own, ("seq", "ch"), ways)
    two = lax.ppermute(own, ("seq", "ch"), [(b, a) for a, b in ways])

    partial = pl.pallas_call(
        functools.partial(kernel, plan, count),
        out_shape=jax.ShapeDtypeStruct((plan.rows, outs), F32),
        in_specs=[vmem] * 6 + [hbm],
        out_specs=vmem,
        scratch_shapes=[
            pltpu.VMEM(head_weight.shape, BF16),
            pltpu.VMEM((STRANDS, plan.hot_rows, plan.depth), BF16),
            pltpu.VMEM((STRANDS, plan.track_rows, plan.depth), BF16),
            pltpu.VMEM((STRANDS * plan.track_rows, channels), BF16),
            pltpu.VMEM((STRANDS, plan.track_rows, outs), F32),
            pltpu.SemaphoreType.DMA,
        ],
        compiler_params=pltpu.CompilerParams(vmem_limit_bytes=24 * MIB),
        cost_estimate=pl.CostEstimate(flops=8 * 10**9, bytes_accessed=10**7, transcendentals=0),
        name="annotate",
    )(one, own_here, two, weights, mixers, edges, stay(head_weight))

    ring = [(i, (i + 1) % cores) for i in range(cores)]
    total, moving = partial, partial
    for _ in range(cores - 1):
        moving = lax.ppermute(moving, "ch", ring)
        total = total + moving
    return total.astype(BF16)


def solution(mesh):
    in_specs = (
        P(("groups", "seq")),
        P(None, None, "ch"),
        P(None, None, "ch"),
        P("ch", None),
        P(None, "ch", None),
    )
    out_specs = P(("groups", "seq"), None)
    return jax.shard_map(shards, mesh=mesh, in_specs=in_specs, out_specs=out_specs, check_vma=False)
```

```python
import functools

import jax
import jax.numpy as jnp
from jax import lax
from jax.experimental import pallas as pl
from jax.experimental.pallas import tpu as pltpu
from jax.sharding import PartitionSpec as P

LANES = 128
HALF = 64
WIDE = 256
SUB = 8
PACK = 16
LETTERS = 4
STRANDS = 2
PARTS = 2
F32 = jnp.float32
BF16 = jnp.bfloat16
MIB = 1024 * 1024


def up(value, step):
    return -(-value // step) * step


def iota(shape, dim):
    return lax.broadcasted_iota(jnp.int32, shape, dim)


def dot(a, b):
    return jnp.dot(a, b, preferred_element_type=F32)


def ones_where(mask):
    return mask.astype(F32).astype(BF16)


class Plan:
    def __init__(self, rows, short_len, taps, head_taps):
        self.rows, self.short_len, self.taps, self.head_taps = rows, short_len, taps, head_taps
        self.rim = (head_taps - 1) // 2
        self.part = rows // PARTS
        self.window = 2 * taps
        self.offset = self.window - self.part - 2 * self.rim
        self.missing = taps - 1 - self.offset
        self.mix_rows = up(self.part + 2 * self.rim, PACK)
        self.track_rows = (PARTS - 1) * self.part + self.mix_rows
        self.hot_rows = PACK + (PARTS - 1) * self.part + self.window
        self.lead = PACK + self.offset + self.rim + short_len - 1
        self.query_lead = PACK + self.offset
        self.width = up(self.query_lead + self.track_rows + short_len, LANES)
        self.depth = 2 * LETTERS * up(short_len, 2)


def build_weights(plan, nuc_ref, sf_ref, wn_ref):
    row = iota((2 * LETTERS, WIDE), 0)
    first = row < LETTERS
    short_len = plan.short_len

    def step(v, carry):
        lanes = pl.ds(pl.multiple_of(v * WIDE, WIDE), WIDE)
        for m in range(3):
            nuc = nuc_ref[m, :, lanes].astype(F32)
            nuc = jnp.concatenate([nuc, nuc], axis=0)
            taps = sf_ref[m, :, lanes]
            pieces = []
            for lag in range(0, short_len, 2):
                a = jnp.broadcast_to(taps[lag : lag + 1], row.shape)
                if lag + 1 < short_len:
                    b = jnp.broadcast_to(taps[lag + 1 : lag + 2], row.shape)
                else:
                    b = jnp.zeros(row.shape, F32)
                pieces.append(jnp.where(first, a, b) * nuc)
            product = jnp.concatenate(pieces, axis=0)
            high = product.astype(BF16)
            low = (product - high.astype(F32)).astype(BF16)
            wn_ref[m, :, lanes] = jnp.concatenate([high, low], axis=0)
        return carry

    lax.fori_loop(0, nuc_ref.shape[2] // WIDE, step, 0)


def build_mixers(plan, mr_ref, fr_ref, mixer_ref):
    taps, rows = plan.taps, plan.mix_rows
    total = iota((taps, taps), 0) + iota((taps, taps), 1)
    turn = (total == plan.offset) | (total == plan.offset + taps)
    fr_ref[...] = dot(mr_ref[...].astype(BF16), ones_where(turn))
    gap = iota((rows, taps), 0) - iota((rows, taps), 1)
    near_mask = ones_where((gap <= plan.missing) & (gap >= -plan.offset))
    far_mask = ones_where(gap > plan.missing)
    filters = mr_ref.shape[0]

    def step(b, carry):
        block = fr_ref[pl.ds(pl.multiple_of(b * SUB, SUB), SUB), :]
        for g in range(SUB):
            wide = jnp.broadcast_to(block[g : g + 1], (taps, taps))
            turned = pltpu.roll(wide, 0, 1, stride=1, stride_axis=0).astype(BF16)
            turned = jnp.concatenate([turned, turned[: rows - taps]], axis=0)
            at = pl.ds(pl.multiple_of((b * SUB + g) * rows, rows), rows)
            mixer_ref[at, :taps] = turned * near_mask
            mixer_ref[at, taps:] = turned * far_mask
        return carry

    lax.fori_loop(0, filters // SUB, step, 0)


def build_edges(plan, mr_ref, edge_ref):
    filters, taps = mr_ref.shape
    channels = edge_ref.shape[1]
    rows = edge_ref.shape[0]
    row, tap = iota((rows, taps), 0), iota((rows, taps), 1)
    wanted = tap == row % SUB + plan.offset + 1 + row // SUB
    picked = lax.dot_general(
        ones_where(wanted), mr_ref[...].astype(BF16), (((1,), (1,)), ((), ())), preferred_element_type=F32
    ).astype(BF16)
    width = channels // filters

    def step(v, carry):
        shape = (filters, WIDE)
        spread = ones_where(iota(shape, 0) == (iota(shape, 1) + v * WIDE) // width)
        edge_ref[:, pl.ds(pl.multiple_of(v * WIDE, WIDE), WIDE)] = dot(picked, spread)
        return carry

    lax.fori_loop(0, channels // WIDE, step, 0)


def prepare(
    plan, own_hbm, nuc_hbm, sf_hbm, mr_hbm, own_ref, wn_ref, mixer_ref, edge_ref,
    nuc_ref, sf_ref, mr_ref, fr_ref, sems,
):
    pairs = [(mr_hbm, mr_ref), (nuc_hbm, nuc_ref), (sf_hbm, sf_ref), (own_hbm, own_ref)]
    copies = [pltpu.make_async_copy(a, b, sems.at[i]) for i, (a, b) in enumerate(pairs)]
    for copy in copies:
        copy.start()
    copies[0].wait()
    build_mixers(plan, mr_ref, fr_ref, mixer_ref)
    build_edges(plan, mr_ref, edge_ref)
    for copy in copies[1:]:
        copy.wait()
    build_weights(plan, nuc_ref, sf_ref, wn_ref)


def coded_letters(plan, count, one_ref, own_ref, two_ref):
    place = lax.axis_index("seq")
    onward = lax.rem(place + lax.axis_index("ch"), 2) == 0
    one, two = one_ref[...], two_ref[...]
    before = jnp.where(onward, one, two) + 1
    after = jnp.where(onward, two, one) + 1
    before = jnp.where(place > 0, before, 0)
    after = jnp.where(place < count - 1, after, 0)
    around = jnp.concatenate([before, own_ref[...] + 1, after], axis=1)
    blocks = around.shape[1] // LANES
    pieces = [around[:, i * LANES : (i + 1) * LANES] for i in range(blocks)]
    pieces += [jnp.zeros_like(pieces[0])] * (up(blocks, SUB) - blocks)
    flip = ones_where(iota((LANES, LANES), 0) + iota((LANES, LANES), 1) == LANES - 1)
    turned = dot(jnp.concatenate(pieces, axis=0).astype(F32).astype(BF16), flip).astype(jnp.int32)
    back = jnp.concatenate([turned[i : i + 1] for i in reversed(range(blocks))], axis=1)
    back = jnp.where(back > 0, LETTERS + 1 - back, 0)
    rest = jnp.zeros((SUB - STRANDS, around.shape[1]), jnp.int32)
    return jnp.concatenate([around, back, rest], axis=0)


def build_onehot(plan, tok, hot_ref, query_ref):
    width = tok.shape[1]
    hot_lanes, query_lanes = up(plan.hot_rows, LANES), up(plan.track_rows, LANES)
    lags = []
    for lag in range(plan.short_len):
        lead = plan.rows - plan.lead + plan.short_len - 1 - lag
        a = pltpu.roll(tok, (width - lead) % width, 1)[:, :hot_lanes]
        b = pltpu.roll(tok, (width - lead - plan.query_lead) % width, 1)[:, :query_lanes]
        lags.append(jnp.concatenate([a, b], axis=1))
    own = lags[0] > 0
    zero = jnp.zeros_like(lags[0])
    lags = [jnp.where(own, lag, zero) for lag in lags]
    if len(lags) % 2:
        lags.append(zero)
    row = iota((2 * LETTERS, zero.shape[1]), 0)
    first = row < LETTERS
    letter = jnp.where(first, row, row - LETTERS) + 1
    for s in range(STRANDS):
        pieces = []
        for lag in range(0, len(lags), 2):
            a = jnp.broadcast_to(lags[lag][s : s + 1], row.shape)
            b = jnp.broadcast_to(lags[lag + 1][s : s + 1], row.shape)
            pieces.append((jnp.where(first, a, b) == letter).astype(F32))
        hot = jnp.concatenate(pieces + pieces, axis=0).T.astype(BF16)
        hot_ref[s] = hot[: plan.hot_rows]
        query_ref[s] = hot[hot_lanes : hot_lanes + plan.track_rows]


def kernel(
    plan, count, one_ref, own_ref, two_ref, wn_ref, mixer_ref, edge_ref, hw_hbm, out_ref,
    hw_ref, hot_ref, query_ref, data_now, edge_now, query_now, track_ref, score_ref, sem,
):
    channels = wn_ref.shape[2]
    part, window, mix_rows = plan.part, plan.window, plan.mix_rows
    group_width = channels * mix_rows // mixer_ref.shape[0]
    tile_groups = HALF // group_width
    tile_rows = tile_groups * mix_rows

    fetch = pltpu.make_async_copy(hw_hbm, hw_ref, sem)
    fetch.start()
    tok = coded_letters(plan, count, one_ref, own_ref, two_ref)
    build_onehot(plan, tok, hot_ref, query_ref)

    lane_group = (iota((mix_rows, WIDE), 1) % HALF) // group_width
    low_half = iota((window, LANES), 1) < HALF
    low_mix = low_half[:mix_rows]

    steps = channels // WIDE

    def gate(v, s):
        lanes = pl.ds(v * WIDE, WIDE)
        slot = v % 2
        hot = hot_ref[s]
        gated = dot(hot, wn_ref[1, :, lanes]) * dot(hot, wn_ref[2, :, lanes])
        query_now[slot, s] = dot(query_ref[s], wn_ref[0, :, lanes])
        for p in range(PARTS):
            at = PACK + p * part
            edge_now[slot, s, p] = gated[at - SUB : at]
        for j in range(WIDE // LANES):
            some = slice(j * LANES, (j + 1) * LANES)
            a = gated[PACK : PACK + window, some]
            b = pltpu.roll(gated[PACK + part : PACK + part + window, some], HALF, 1)
            to = slice(s * LANES, (s + 1) * LANES)
            data_now[slot, 2 * j, :, to] = jnp.where(low_half, a, b).astype(BF16)
            data_now[slot, 2 * j + 1, :, to] = jnp.where(low_half, b, a).astype(BF16)

    def mix(v, j):
        slot = v % 2
        some = slice(j * LANES, (j + 1) * LANES)
        to = pl.ds(v * WIDE + j * LANES, LANES)
        mixed = []
        for h in range(2):
            tile = v * (WIDE // HALF) + 2 * j + h
            mixers = mixer_ref[pl.ds(tile * tile_rows, tile_rows), :]
            data = data_now[slot, 2 * j + h]
            middle = tile_rows // 2
            pieces = jnp.concatenate([dot(mixers[:middle], data), dot(mixers[middle:], data)], axis=0)
            chosen = pieces[:mix_rows]
            for g in range(1, tile_groups):
                chosen = jnp.where(lane_group == g, pieces[g * mix_rows : (g + 1) * mix_rows], chosen)
            mixed.append(chosen)
        for s in range(STRANDS):
            a, b = (m[:, s * LANES : (s + 1) * LANES] for m in mixed)
            both = [jnp.where(low_mix, a, b), pltpu.roll(jnp.where(low_mix, b, a), HALF, 1)]
            for p in range(PARTS):
                fix = both[p][:SUB]
                for d in range(plan.missing):
                    base = edge_now[slot, s, p, SUB - 1 - d : SUB - d, some]
                    fix = fix + edge_ref[d * SUB : (d + 1) * SUB, to] * base
                length = part if p < PARTS - 1 else mix_rows
                whole = jnp.concatenate([fix, both[p][SUB:length]], axis=0)
                own = query_now[slot, s, p * part : p * part + length, some]
                at = s * plan.track_rows + p * part
                track_ref[at : at + length, to] = (own * whole).astype(BF16)

    for s in range(STRANDS):
        gate(0, s)
    for v in range(steps):
        for i in range(2):
            if v + 1 < steps:
                gate(v + 1, i)
            mix(v, i)

    fetch.wait()
    totals = [None, None]
    for k in range(plan.head_taps):
        score = dot(track_ref[...], hw_ref[k])
        for s in range(STRANDS):
            score_ref[s] = score[s * plan.track_rows : (s + 1) * plan.track_rows]
            shifted = score_ref[s, k : k + plan.rows]
            totals[s] = shifted if k == 0 else totals[s] + shifted
    forward, backward = totals
    flip = ones_where(iota((plan.rows, plan.rows), 0) + iota((plan.rows, plan.rows), 1) == plan.rows - 1)
    for _ in range(3):
        high = backward.astype(BF16)
        forward = forward + dot(flip, high)
        backward = backward - high.astype(F32)
    out_ref[...] = forward


def neighbour_ways(count, cores):
    ways = []
    for i in range(count):
        for c in range(cores):
            step = 1 if (i + c) % 2 == 0 else -1
            there = (i + step, c ^ 1) if 0 <= i + step < count else (i, c ^ 1)
            ways.append((i * cores + c, there[0] * cores + there[1]))
    return ways


def stay(array):
    return pltpu.with_memory_space_constraint(array, pltpu.HBM)


def shards(tokens, nuc_table, short_filter, mr_filter, head_weight):
    _, short_len, channels = short_filter.shape
    filters, taps = mr_filter.shape
    head_taps, _, outs = head_weight.shape
    plan = Plan(tokens.shape[0], short_len, taps, head_taps)
    vmem = pl.BlockSpec(memory_space=pltpu.VMEM)
    hbm = pl.BlockSpec(memory_space=pl.ANY)

    own = tokens.reshape(1, plan.rows)
    own_here, weights, mixers, edges = pl.pallas_call(
        functools.partial(prepare, plan),
        out_shape=(
            jax.ShapeDtypeStruct(own.shape, own.dtype),
            jax.ShapeDtypeStruct((3, plan.depth, channels), BF16),
            jax.ShapeDtypeStruct((filters * plan.mix_rows, plan.window), BF16),
            jax.ShapeDtypeStruct((up(plan.missing, 1) * SUB, channels), F32),
        ),
        in_specs=[hbm] * 4,
        out_specs=(vmem,) * 4,
        scratch_shapes=[
            pltpu.VMEM(nuc_table.shape, BF16),
            pltpu.VMEM(short_filter.shape, F32),
            pltpu.VMEM(mr_filter.shape, F32),
            pltpu.VMEM(mr_filter.shape, F32),
            pltpu.SemaphoreType.DMA((4,)),
        ],
        compiler_params=pltpu.CompilerParams(vmem_limit_bytes=16 * MIB),
        cost_estimate=pl.CostEstimate(flops=10**8, bytes_accessed=10**7, transcendentals=0),
        name="prepare",
    )(*(stay(a) for a in (own, nuc_table, short_filter, mr_filter)))

    count, cores = lax.axis_size("seq"), lax.axis_size("ch")
    ways = neighbour_ways(count, cores)
    one = lax.ppermute(own, ("seq", "ch"), ways)
    two = lax.ppermute(own, ("seq", "ch"), [(b, a) for a, b in ways])

    partial = pl.pallas_call(
        functools.partial(kernel, plan, count),
        out_shape=jax.ShapeDtypeStruct((plan.rows, outs), F32),
        in_specs=[vmem] * 6 + [hbm],
        out_specs=vmem,
        scratch_shapes=[
            pltpu.VMEM(head_weight.shape, BF16),
            pltpu.VMEM((STRANDS, plan.hot_rows, plan.depth), BF16),
            pltpu.VMEM((STRANDS, plan.track_rows, plan.depth), BF16),
            pltpu.VMEM((2, WIDE // HALF, plan.window, WIDE), BF16),
            pltpu.VMEM((2, STRANDS, PARTS, SUB, WIDE), F32),
            pltpu.VMEM((2, STRANDS, plan.track_rows, WIDE), F32),
            pltpu.VMEM((STRANDS * plan.track_rows, channels), BF16),
            pltpu.VMEM((STRANDS, plan.track_rows, outs), F32),
            pltpu.SemaphoreType.DMA,
        ],
        compiler_params=pltpu.CompilerParams(vmem_limit_bytes=24 * MIB),
        cost_estimate=pl.CostEstimate(flops=8 * 10**9, bytes_accessed=10**7, transcendentals=0),
        name="annotate",
    )(one, own_here, two, weights, mixers, edges, stay(head_weight))

    ring = [(i, (i + 1) % cores) for i in range(cores)]
    total, moving = partial, partial
    for _ in range(cores - 1):
        moving = lax.ppermute(moving, "ch", ring)
        total = total + moving
    return total.astype(BF16)


def solution(mesh):
    in_specs = (
        P(("groups", "seq")),
        P(None, None, "ch"),
        P(None, None, "ch"),
        P("ch", None),
        P(None, "ch", None),
    )
    out_specs = P(("groups", "seq"), None)
    return jax.shard_map(shards, mesh=mesh, in_specs=in_specs, out_specs=out_specs, check_vma=False)
```

```python
import functools

import jax
import jax.numpy as jnp
from jax import lax
from jax.experimental import pallas as pl
from jax.experimental.pallas import tpu as pltpu
from jax.sharding import PartitionSpec as P

LANES = 128
HALF = 64
WIDE = 256
SUB = 8
PACK = 16
LETTERS = 4
STRANDS = 2
PARTS = 2
F32 = jnp.float32
BF16 = jnp.bfloat16
MIB = 1024 * 1024


def up(value, step):
    return -(-value // step) * step


def iota(shape, dim):
    return lax.broadcasted_iota(jnp.int32, shape, dim)


def dot(a, b):
    return jnp.dot(a, b, preferred_element_type=F32)


def ones_where(mask):
    return mask.astype(F32).astype(BF16)


class Plan:
    def __init__(self, rows, short_len, taps, head_taps):
        self.rows, self.short_len, self.taps, self.head_taps = rows, short_len, taps, head_taps
        self.rim = (head_taps - 1) // 2
        self.part = rows // PARTS
        self.window = 2 * taps
        self.offset = self.window - self.part - 2 * self.rim
        self.missing = taps - 1 - self.offset
        self.mix_rows = up(self.part + 2 * self.rim, SUB)
        self.track_rows = (PARTS - 1) * self.part + self.mix_rows
        self.hot_rows = PACK + (PARTS - 1) * self.part + self.window
        self.lead = PACK + self.offset + self.rim + short_len - 1
        self.query_lead = PACK + self.offset
        self.width = up(self.query_lead + self.track_rows + short_len, LANES)
        self.depth = 2 * LETTERS * up(short_len, 2)


def build_weights(plan, nuc_ref, sf_ref, wn_ref):
    row = iota((2 * LETTERS, WIDE), 0)
    first = row < LETTERS
    short_len = plan.short_len

    def step(v, carry):
        lanes = pl.ds(pl.multiple_of(v * WIDE, WIDE), WIDE)
        for m in range(3):
            nuc = nuc_ref[m, :, lanes].astype(F32)
            nuc = jnp.concatenate([nuc, nuc], axis=0)
            taps = sf_ref[m, :, lanes]
            pieces = []
            for lag in range(0, short_len, 2):
                a = jnp.broadcast_to(taps[lag : lag + 1], row.shape)
                if lag + 1 < short_len:
                    b = jnp.broadcast_to(taps[lag + 1 : lag + 2], row.shape)
                else:
                    b = jnp.zeros(row.shape, F32)
                pieces.append(jnp.where(first, a, b) * nuc)
            product = jnp.concatenate(pieces, axis=0)
            high = product.astype(BF16)
            low = (product - high.astype(F32)).astype(BF16)
            wn_ref[m, :, lanes] = jnp.concatenate([high, low], axis=0)
        return carry

    lax.fori_loop(0, nuc_ref.shape[2] // WIDE, step, 0)


def build_turned(plan, mr_ref, fr_ref):
    total = iota((plan.taps, plan.taps), 0) + iota((plan.taps, plan.taps), 1)
    turn = (total == plan.offset) | (total == plan.offset + plan.taps)
    fr_ref[...] = dot(mr_ref[...].astype(BF16), ones_where(turn))


def build_masks(plan, mask_ref):
    taps = plan.taps
    gap = iota((plan.mix_rows, taps), 0) - iota((plan.mix_rows, taps), 1)
    mask_ref[:, :taps] = ones_where((gap <= plan.missing) & (gap >= -plan.offset))
    mask_ref[:, taps:] = ones_where(gap > plan.missing)


def build_mixer(plan, taps_row, mask_ref):
    taps = plan.taps
    wide = jnp.broadcast_to(taps_row, (taps, taps))
    turned = pltpu.roll(wide, 0, 1, stride=1, stride_axis=0).astype(BF16)
    turned = jnp.concatenate([turned, turned[: plan.mix_rows - taps]], axis=0)
    return turned * mask_ref[:, :taps], turned * mask_ref[:, taps:]


def build_edges(plan, mr_ref, edge_ref):
    filters, taps = mr_ref.shape
    channels = edge_ref.shape[1]
    rows = edge_ref.shape[0]
    row, tap = iota((rows, taps), 0), iota((rows, taps), 1)
    wanted = tap == row % SUB + plan.offset + 1 + row // SUB
    picked = lax.dot_general(
        ones_where(wanted), mr_ref[...].astype(BF16), (((1,), (1,)), ((), ())), preferred_element_type=F32
    ).astype(BF16)
    width = channels // filters

    def step(v, carry):
        shape = (filters, WIDE)
        spread = ones_where(iota(shape, 0) == (iota(shape, 1) + v * WIDE) // width)
        edge_ref[:, pl.ds(pl.multiple_of(v * WIDE, WIDE), WIDE)] = dot(picked, spread)
        return carry

    lax.fori_loop(0, channels // WIDE, step, 0)


def prepare(
    plan, own_hbm, nuc_hbm, sf_hbm, mr_hbm, own_ref, wn_ref, fr_ref, edge_ref,
    nuc_ref, sf_ref, mr_ref, sems,
):
    pairs = [(mr_hbm, mr_ref), (nuc_hbm, nuc_ref), (sf_hbm, sf_ref), (own_hbm, own_ref)]
    copies = [pltpu.make_async_copy(a, b, sems.at[i]) for i, (a, b) in enumerate(pairs)]
    for copy in copies:
        copy.start()
    copies[0].wait()
    build_turned(plan, mr_ref, fr_ref)
    build_edges(plan, mr_ref, edge_ref)
    for copy in copies[1:]:
        copy.wait()
    build_weights(plan, nuc_ref, sf_ref, wn_ref)


def coded_letters(plan, count, one_ref, own_ref, two_ref):
    place = lax.axis_index("seq")
    onward = lax.rem(place + lax.axis_index("ch"), 2) == 0
    one, two = one_ref[...], two_ref[...]
    before = jnp.where(onward, one, two) + 1
    after = jnp.where(onward, two, one) + 1
    before = jnp.where(place > 0, before, 0)
    after = jnp.where(place < count - 1, after, 0)
    around = jnp.concatenate([before, own_ref[...] + 1, after], axis=1)
    blocks = around.shape[1] // LANES
    pieces = [around[:, i * LANES : (i + 1) * LANES] for i in range(blocks)]
    pieces += [jnp.zeros_like(pieces[0])] * (up(blocks, SUB) - blocks)
    flip = ones_where(iota((LANES, LANES), 0) + iota((LANES, LANES), 1) == LANES - 1)
    turned = dot(jnp.concatenate(pieces, axis=0).astype(F32).astype(BF16), flip).astype(jnp.int32)
    back = jnp.concatenate([turned[i : i + 1] for i in reversed(range(blocks))], axis=1)
    back = jnp.where(back > 0, LETTERS + 1 - back, 0)
    rest = jnp.zeros((SUB - STRANDS, around.shape[1]), jnp.int32)
    return jnp.concatenate([around, back, rest], axis=0)


def build_onehot(plan, tok, hot_ref, query_ref):
    width = tok.shape[1]
    hot_lanes, query_lanes = up(plan.hot_rows, LANES), up(plan.track_rows, LANES)
    lags = []
    for lag in range(plan.short_len):
        lead = plan.rows - plan.lead + plan.short_len - 1 - lag
        a = pltpu.roll(tok, (width - lead) % width, 1)[:, :hot_lanes]
        b = pltpu.roll(tok, (width - lead - plan.query_lead) % width, 1)[:, :query_lanes]
        lags.append(jnp.concatenate([a, b], axis=1))
    own = lags[0] > 0
    zero = jnp.zeros_like(lags[0])
    lags = [jnp.where(own, lag, zero) for lag in lags]
    if len(lags) % 2:
        lags.append(zero)
    row = iota((2 * LETTERS, zero.shape[1]), 0)
    first = row < LETTERS
    letter = jnp.where(first, row, row - LETTERS) + 1
    for s in range(STRANDS):
        pieces = []
        for lag in range(0, len(lags), 2):
            a = jnp.broadcast_to(lags[lag][s : s + 1], row.shape)
            b = jnp.broadcast_to(lags[lag + 1][s : s + 1], row.shape)
            pieces.append((jnp.where(first, a, b) == letter).astype(F32))
        hot = jnp.concatenate(pieces + pieces, axis=0).T.astype(BF16)
        hot_ref[s] = hot[: plan.hot_rows]
        query_ref[s] = hot[hot_lanes : hot_lanes + plan.track_rows]


def kernel(
    plan, count, one_ref, own_ref, two_ref, wn_ref, fr_ref, edge_ref, hw_hbm, out_ref,
    hw_ref, hot_ref, query_ref, mask_ref, mixer_now, data_now, edge_now, query_now, track_ref, score_ref, sem,
):
    channels = wn_ref.shape[2]
    part, window, mix_rows = plan.part, plan.window, plan.mix_rows
    group_width = channels // fr_ref.shape[0]
    half_step = WIDE // group_width // 2
    tile_groups = HALF // group_width
    tile_rows = tile_groups * mix_rows

    fetch = pltpu.make_async_copy(hw_hbm, hw_ref, sem)
    fetch.start()
    build_masks(plan, mask_ref)
    tok = coded_letters(plan, count, one_ref, own_ref, two_ref)
    build_onehot(plan, tok, hot_ref, query_ref)

    lane_group = (iota((mix_rows, WIDE), 1) % HALF) // group_width
    low_half = iota((window, LANES), 1) < HALF
    low_mix = low_half[:mix_rows]

    steps = channels // WIDE

    def gate(v, slot, s):
        lanes = pl.ds(pl.multiple_of(v * WIDE, WIDE), WIDE)
        hot = hot_ref[s]
        gated = dot(hot, wn_ref[1, :, lanes]) * dot(hot, wn_ref[2, :, lanes])
        query_now[slot, s] = dot(query_ref[s], wn_ref[0, :, lanes])
        for p in range(PARTS):
            at = PACK + p * part
            edge_now[slot, s, p] = gated[at - SUB : at]
        for j in range(WIDE // LANES):
            some = slice(j * LANES, (j + 1) * LANES)
            a = gated[PACK : PACK + window, some]
            b = pltpu.roll(gated[PACK + part : PACK + part + window, some], HALF, 1)
            to = slice(s * LANES, (s + 1) * LANES)
            data_now[slot, 2 * j, :, to] = jnp.where(low_half, a, b).astype(BF16)
            data_now[slot, 2 * j + 1, :, to] = jnp.where(low_half, b, a).astype(BF16)

    def arrange(v, slot, i):
        first = pl.multiple_of((2 * v + i) * half_step, half_step)
        block = fr_ref[pl.ds(first, half_step), :]
        for g in range(half_step):
            near, far = build_mixer(plan, block[g : g + 1], mask_ref)
            at = (i * half_step + g) * mix_rows
            mixer_now[slot, at : at + mix_rows, : plan.taps] = near
            mixer_now[slot, at : at + mix_rows, plan.taps :] = far

    def mix(v, slot, j):
        some = slice(j * LANES, (j + 1) * LANES)
        to = pl.ds(pl.multiple_of(v * WIDE + j * LANES, LANES), LANES)
        mixed = []
        for h in range(2):
            at = (2 * j + h) * tile_rows
            mixers = mixer_now[slot, at : at + tile_rows, :]
            data = data_now[slot, 2 * j + h]
            middle = tile_rows // 2
            pieces = jnp.concatenate([dot(mixers[:middle], data), dot(mixers[middle:], data)], axis=0)
            chosen = pieces[:mix_rows]
            for g in range(1, tile_groups):
                chosen = jnp.where(lane_group == g, pieces[g * mix_rows : (g + 1) * mix_rows], chosen)
            mixed.append(chosen)
        for s in range(STRANDS):
            a, b = (m[:, s * LANES : (s + 1) * LANES] for m in mixed)
            both = [jnp.where(low_mix, a, b), pltpu.roll(jnp.where(low_mix, b, a), HALF, 1)]
            for p in range(PARTS):
                fix = both[p][:SUB]
                for d in range(plan.missing):
                    base = edge_now[slot, s, p, SUB - 1 - d : SUB - d, some]
                    fix = fix + edge_ref[d * SUB : (d + 1) * SUB, to] * base
                length = part if p < PARTS - 1 else mix_rows
                whole = jnp.concatenate([fix, both[p][SUB:length]], axis=0)
                own = query_now[slot, s, p * part : p * part + length, some]
                at = s * plan.track_rows + p * part
                track_ref[at : at + length, to] = (own * whole).astype(BF16)

    for s in range(STRANDS):
        gate(0, 0, s)
        arrange(0, 0, s)

    def pair(u, carry):
        for slot in range(2):
            v = 2 * u + slot
            following = jnp.minimum(v + 1, steps - 1)
            for i in range(2):
                gate(following, 1 - slot, i)
                arrange(following, 1 - slot, i)
                mix(v, slot, i)
        return carry

    lax.fori_loop(0, steps // 2, pair, 0)

    fetch.wait()
    totals = [None, None]
    for k in range(plan.head_taps):
        score = dot(track_ref[...], hw_ref[k])
        for s in range(STRANDS):
            score_ref[s] = score[s * plan.track_rows : (s + 1) * plan.track_rows]
            shifted = score_ref[s, k : k + plan.rows]
            totals[s] = shifted if k == 0 else totals[s] + shifted
    forward, backward = totals
    flip = ones_where(iota((plan.rows, plan.rows), 0) + iota((plan.rows, plan.rows), 1) == plan.rows - 1)
    for _ in range(3):
        high = backward.astype(BF16)
        forward = forward + dot(flip, high)
        backward = backward - high.astype(F32)
    out_ref[...] = forward


def neighbour_ways(count, cores):
    ways = []
    for i in range(count):
        for c in range(cores):
            step = 1 if (i + c) % 2 == 0 else -1
            there = (i + step, c ^ 1) if 0 <= i + step < count else (i, c ^ 1)
            ways.append((i * cores + c, there[0] * cores + there[1]))
    return ways


def stay(array):
    return pltpu.with_memory_space_constraint(array, pltpu.HBM)


def shards(tokens, nuc_table, short_filter, mr_filter, head_weight):
    _, short_len, channels = short_filter.shape
    filters, taps = mr_filter.shape
    head_taps, _, outs = head_weight.shape
    plan = Plan(tokens.shape[0], short_len, taps, head_taps)
    vmem = pl.BlockSpec(memory_space=pltpu.VMEM)
    hbm = pl.BlockSpec(memory_space=pl.ANY)

    own = tokens.reshape(1, plan.rows)
    own_here, weights, turned, edges = pl.pallas_call(
        functools.partial(prepare, plan),
        out_shape=(
            jax.ShapeDtypeStruct(own.shape, own.dtype),
            jax.ShapeDtypeStruct((3, plan.depth, channels), BF16),
            jax.ShapeDtypeStruct(mr_filter.shape, F32),
            jax.ShapeDtypeStruct((up(plan.missing, 1) * SUB, channels), F32),
        ),
        in_specs=[hbm] * 4,
        out_specs=(vmem,) * 4,
        scratch_shapes=[
            pltpu.VMEM(nuc_table.shape, BF16),
            pltpu.VMEM(short_filter.shape, F32),
            pltpu.VMEM(mr_filter.shape, F32),
            pltpu.SemaphoreType.DMA((4,)),
        ],
        compiler_params=pltpu.CompilerParams(vmem_limit_bytes=16 * MIB),
        cost_estimate=pl.CostEstimate(flops=10**8, bytes_accessed=10**7, transcendentals=0),
        name="prepare",
    )(*(stay(a) for a in (own, nuc_table, short_filter, mr_filter)))

    count, cores = lax.axis_size("seq"), lax.axis_size("ch")
    ways = neighbour_ways(count, cores)
    one = lax.ppermute(own, ("seq", "ch"), ways)
    two = lax.ppermute(own, ("seq", "ch"), [(b, a) for a, b in ways])

    partial = pl.pallas_call(
        functools.partial(kernel, plan, count),
        out_shape=jax.ShapeDtypeStruct((plan.rows, outs), F32),
        in_specs=[vmem] * 6 + [hbm],
        out_specs=vmem,
        scratch_shapes=[
            pltpu.VMEM(head_weight.shape, BF16),
            pltpu.VMEM((STRANDS, plan.hot_rows, plan.depth), BF16),
            pltpu.VMEM((STRANDS, plan.track_rows, plan.depth), BF16),
            pltpu.VMEM((plan.mix_rows, plan.window), BF16),
            pltpu.VMEM((2, WIDE * filters // channels * plan.mix_rows, plan.window), BF16),
            pltpu.VMEM((2, WIDE // HALF, plan.window, WIDE), BF16),
            pltpu.VMEM((2, STRANDS, PARTS, SUB, WIDE), F32),
            pltpu.VMEM((2, STRANDS, plan.track_rows, WIDE), F32),
            pltpu.VMEM((STRANDS * plan.track_rows, channels), BF16),
            pltpu.VMEM((STRANDS, plan.track_rows, outs), F32),
            pltpu.SemaphoreType.DMA,
        ],
        compiler_params=pltpu.CompilerParams(vmem_limit_bytes=24 * MIB),
        cost_estimate=pl.CostEstimate(flops=8 * 10**9, bytes_accessed=10**7, transcendentals=0),
        name="annotate",
    )(one, own_here, two, weights, turned, edges, stay(head_weight))

    ring = [(i, (i + 1) % cores) for i in range(cores)]
    total, moving = partial, partial
    for _ in range(cores - 1):
        moving = lax.ppermute(moving, "ch", ring)
        total = total + moving
    return total.astype(BF16)


def solution(mesh):
    in_specs = (
        P(("groups", "seq")),
        P(None, None, "ch"),
        P(None, None, "ch"),
        P("ch", None),
        P(None, "ch", None),
    )
    out_specs = P(("groups", "seq"), None)
    return jax.shard_map(shards, mesh=mesh, in_specs=in_specs, out_specs=out_specs, check_vma=False)
```

```python
import functools

import jax
import jax.numpy as jnp
from jax import lax
from jax.experimental import pallas as pl
from jax.experimental.pallas import tpu as pltpu
from jax.sharding import PartitionSpec as P

LANES = 128
HALF = 64
WIDE = 256
SUB = 8
PACK = 16
LETTERS = 4
STRANDS = 2
PARTS = 2
F32 = jnp.float32
BF16 = jnp.bfloat16
MIB = 1024 * 1024


def up(value, step):
    return -(-value // step) * step


def iota(shape, dim):
    return lax.broadcasted_iota(jnp.int32, shape, dim)


def dot(a, b):
    return jnp.dot(a, b, preferred_element_type=F32)


def ones_where(mask):
    return mask.astype(F32).astype(BF16)


class Plan:
    def __init__(self, rows, short_len, taps, head_taps):
        self.rows, self.short_len, self.taps, self.head_taps = rows, short_len, taps, head_taps
        self.rim = (head_taps - 1) // 2
        self.part = rows // PARTS
        self.window = 2 * taps
        self.offset = self.window - self.part - 2 * self.rim
        self.missing = taps - 1 - self.offset
        self.mix_rows = up(self.part + 2 * self.rim, SUB)
        self.track_rows = (PARTS - 1) * self.part + self.mix_rows
        self.hot_rows = PACK + (PARTS - 1) * self.part + self.window
        self.lead = PACK + self.offset + self.rim + short_len - 1
        self.query_lead = PACK + self.offset
        self.width = up(self.query_lead + self.track_rows + short_len, LANES)
        self.depth = 2 * LETTERS * up(short_len, 2)


def build_weights(plan, nuc_ref, sf_ref, wn_ref):
    row = iota((2 * LETTERS, WIDE), 0)
    first = row < LETTERS
    short_len = plan.short_len

    def step(v, carry):
        lanes = pl.ds(pl.multiple_of(v * WIDE, WIDE), WIDE)
        for m in range(3):
            nuc = nuc_ref[m, :, lanes].astype(F32)
            nuc = jnp.concatenate([nuc, nuc], axis=0)
            taps = sf_ref[m, :, lanes]
            pieces = []
            for lag in range(0, short_len, 2):
                a = jnp.broadcast_to(taps[lag : lag + 1], row.shape)
                if lag + 1 < short_len:
                    b = jnp.broadcast_to(taps[lag + 1 : lag + 2], row.shape)
                else:
                    b = jnp.zeros(row.shape, F32)
                pieces.append(jnp.where(first, a, b) * nuc)
            product = jnp.concatenate(pieces, axis=0)
            high = product.astype(BF16)
            low = (product - high.astype(F32)).astype(BF16)
            wn_ref[m, :, lanes] = jnp.concatenate([high, low], axis=0)
        return carry

    lax.fori_loop(0, nuc_ref.shape[2] // WIDE, step, 0)


def build_turned(plan, mr_ref, fr_ref):
    total = iota((plan.taps, plan.taps), 0) + iota((plan.taps, plan.taps), 1)
    turn = (total == plan.offset) | (total == plan.offset + plan.taps)
    fr_ref[...] = dot(mr_ref[...].astype(BF16), ones_where(turn))


def build_masks(plan, mask_ref):
    taps = plan.taps
    gap = iota((plan.mix_rows, taps), 0) - iota((plan.mix_rows, taps), 1)
    mask_ref[:, :taps] = ((gap <= plan.missing) & (gap >= -plan.offset)).astype(F32)
    mask_ref[:, taps:] = (gap > plan.missing).astype(F32)


def build_mixer(plan, taps_row, mask_ref):
    taps = plan.taps
    wide = jnp.broadcast_to(taps_row, (taps, taps))
    turned = pltpu.roll(wide, 0, 1, stride=1, stride_axis=0)
    turned = jnp.concatenate([turned, turned[: plan.mix_rows - taps]], axis=0)
    return (jnp.concatenate([turned, turned], axis=1) * mask_ref[...]).astype(BF16)


def build_edges(plan, mr_ref, edge_ref):
    filters, taps = mr_ref.shape
    channels = edge_ref.shape[1]
    rows = edge_ref.shape[0]
    row, tap = iota((rows, taps), 0), iota((rows, taps), 1)
    wanted = tap == row % SUB + plan.offset + 1 + row // SUB
    picked = lax.dot_general(
        ones_where(wanted), mr_ref[...].astype(BF16), (((1,), (1,)), ((), ())), preferred_element_type=F32
    ).astype(BF16)
    width = channels // filters

    def step(v, carry):
        shape = (filters, WIDE)
        spread = ones_where(iota(shape, 0) == (iota(shape, 1) + v * WIDE) // width)
        edge_ref[:, pl.ds(pl.multiple_of(v * WIDE, WIDE), WIDE)] = dot(picked, spread)
        return carry

    lax.fori_loop(0, channels // WIDE, step, 0)


def prepare(
    plan, own_hbm, nuc_hbm, sf_hbm, mr_hbm, own_ref, wn_ref, fr_ref, edge_ref,
    nuc_ref, sf_ref, mr_ref, sems,
):
    pairs = [(mr_hbm, mr_ref), (nuc_hbm, nuc_ref), (sf_hbm, sf_ref), (own_hbm, own_ref)]
    copies = [pltpu.make_async_copy(a, b, sems.at[i]) for i, (a, b) in enumerate(pairs)]
    for copy in copies:
        copy.start()
    copies[0].wait()
    build_turned(plan, mr_ref, fr_ref)
    build_edges(plan, mr_ref, edge_ref)
    for copy in copies[1:]:
        copy.wait()
    build_weights(plan, nuc_ref, sf_ref, wn_ref)


def coded_letters(plan, count, one_ref, own_ref, two_ref):
    place = lax.axis_index("seq")
    onward = lax.rem(place + lax.axis_index("ch"), 2) == 0
    one, two = one_ref[...], two_ref[...]
    before = jnp.where(onward, one, two) + 1
    after = jnp.where(onward, two, one) + 1
    before = jnp.where(place > 0, before, 0)
    after = jnp.where(place < count - 1, after, 0)
    around = jnp.concatenate([before, own_ref[...] + 1, after], axis=1)
    blocks = around.shape[1] // LANES
    pieces = [around[:, i * LANES : (i + 1) * LANES] for i in range(blocks)]
    pieces += [jnp.zeros_like(pieces[0])] * (up(blocks, SUB) - blocks)
    flip = ones_where(iota((LANES, LANES), 0) + iota((LANES, LANES), 1) == LANES - 1)
    turned = dot(jnp.concatenate(pieces, axis=0).astype(F32).astype(BF16), flip).astype(jnp.int32)
    back = jnp.concatenate([turned[i : i + 1] for i in reversed(range(blocks))], axis=1)
    back = jnp.where(back > 0, LETTERS + 1 - back, 0)
    rest = jnp.zeros((SUB - STRANDS, around.shape[1]), jnp.int32)
    return jnp.concatenate([around, back, rest], axis=0)


def build_onehot(plan, tok, hot_ref, query_ref):
    width = tok.shape[1]
    hot_lanes, query_lanes = up(plan.hot_rows, LANES), up(plan.track_rows, LANES)
    lags = []
    for lag in range(plan.short_len):
        lead = plan.rows - plan.lead + plan.short_len - 1 - lag
        a = pltpu.roll(tok, (width - lead) % width, 1)[:, :hot_lanes]
        b = pltpu.roll(tok, (width - lead - plan.query_lead) % width, 1)[:, :query_lanes]
        lags.append(jnp.concatenate([a, b], axis=1))
    own = lags[0] > 0
    zero = jnp.zeros_like(lags[0])
    lags = [jnp.where(own, lag, zero) for lag in lags]
    if len(lags) % 2:
        lags.append(zero)
    row = iota((2 * LETTERS, zero.shape[1]), 0)
    first = row < LETTERS
    letter = jnp.where(first, row, row - LETTERS) + 1
    for s in range(STRANDS):
        pieces = []
        for lag in range(0, len(lags), 2):
            a = jnp.broadcast_to(lags[lag][s : s + 1], row.shape)
            b = jnp.broadcast_to(lags[lag + 1][s : s + 1], row.shape)
            pieces.append((jnp.where(first, a, b) == letter).astype(F32))
        hot = jnp.concatenate(pieces + pieces, axis=0).T.astype(BF16)
        hot_ref[s] = hot[: plan.hot_rows]
        query_ref[s] = hot[hot_lanes : hot_lanes + plan.track_rows]


def kernel(
    plan, count, one_ref, own_ref, two_ref, wn_ref, fr_ref, edge_ref, hw_hbm, out_ref,
    hw_ref, hot_ref, query_ref, mask_ref, mixer_now, data_now, edge_now, query_now, track_ref, score_ref, sem,
):
    channels = wn_ref.shape[2]
    part, window, mix_rows = plan.part, plan.window, plan.mix_rows
    group_width = channels // fr_ref.shape[0]
    half_step = WIDE // group_width // 2
    tile_groups = HALF // group_width
    tile_rows = tile_groups * mix_rows

    fetch = pltpu.make_async_copy(hw_hbm, hw_ref, sem)
    fetch.start()
    build_masks(plan, mask_ref)
    tok = coded_letters(plan, count, one_ref, own_ref, two_ref)
    build_onehot(plan, tok, hot_ref, query_ref)

    lane_group = (iota((mix_rows, WIDE), 1) % HALF) // group_width
    low_half = iota((window, LANES), 1) < HALF
    low_mix = low_half[:mix_rows]

    steps = channels // WIDE

    def gate(v, slot, s):
        lanes = pl.ds(pl.multiple_of(v * WIDE, WIDE), WIDE)
        hot = hot_ref[s]
        gated = dot(hot, wn_ref[1, :, lanes]) * dot(hot, wn_ref[2, :, lanes])
        query_now[slot, s] = dot(query_ref[s], wn_ref[0, :, lanes])
        for p in range(PARTS):
            at = PACK + p * part
            edge_now[slot, s, p] = gated[at - SUB : at]
        for j in range(WIDE // LANES):
            some = slice(j * LANES, (j + 1) * LANES)
            a = gated[PACK : PACK + window, some]
            b = pltpu.roll(gated[PACK + part : PACK + part + window, some], HALF, 1)
            to = slice(s * LANES, (s + 1) * LANES)
            data_now[slot, 2 * j, :, to] = jnp.where(low_half, a, b).astype(BF16)
            data_now[slot, 2 * j + 1, :, to] = jnp.where(low_half, b, a).astype(BF16)

    def arrange(v, slot, i):
        first = pl.multiple_of((2 * v + i) * half_step, half_step)
        block = fr_ref[pl.ds(first, half_step), :]
        for g in range(half_step):
            at = (i * half_step + g) * mix_rows
            mixer_now[slot, at : at + mix_rows, :] = build_mixer(plan, block[g : g + 1], mask_ref)

    def mix(v, slot, j):
        some = slice(j * LANES, (j + 1) * LANES)
        to = pl.ds(pl.multiple_of(v * WIDE + j * LANES, LANES), LANES)
        mixed = []
        for h in range(2):
            at = (2 * j + h) * tile_rows
            mixers = mixer_now[slot, at : at + tile_rows, :]
            data = data_now[slot, 2 * j + h]
            middle = tile_rows // 2
            pieces = jnp.concatenate([dot(mixers[:middle], data), dot(mixers[middle:], data)], axis=0)
            chosen = pieces[:mix_rows]
            for g in range(1, tile_groups):
                chosen = jnp.where(lane_group == g, pieces[g * mix_rows : (g + 1) * mix_rows], chosen)
            mixed.append(chosen)
        for s in range(STRANDS):
            a, b = (m[:, s * LANES : (s + 1) * LANES] for m in mixed)
            both = [jnp.where(low_mix, a, b), pltpu.roll(jnp.where(low_mix, b, a), HALF, 1)]
            for p in range(PARTS):
                fix = both[p][:SUB]
                for d in range(plan.missing):
                    base = edge_now[slot, s, p, SUB - 1 - d : SUB - d, some]
                    fix = fix + edge_ref[d * SUB : (d + 1) * SUB, to] * base
                length = part if p < PARTS - 1 else mix_rows
                whole = jnp.concatenate([fix, both[p][SUB:length]], axis=0)
                own = query_now[slot, s, p * part : p * part + length, some]
                at = s * plan.track_rows + p * part
                track_ref[at : at + length, to] = (own * whole).astype(BF16)

    for s in range(STRANDS):
        gate(0, 0, s)
        arrange(0, 0, s)

    def pair(u, carry):
        for slot in range(2):
            v = 2 * u + slot
            following = jnp.minimum(v + 1, steps - 1)
            for i in range(2):
                gate(following, 1 - slot, i)
                arrange(following, 1 - slot, i)
                mix(v, slot, i)
        return carry

    lax.fori_loop(0, steps // 2, pair, 0)

    fetch.wait()
    totals = [None, None]
    for k in range(plan.head_taps):
        score = dot(track_ref[...], hw_ref[k])
        for s in range(STRANDS):
            score_ref[s] = score[s * plan.track_rows : (s + 1) * plan.track_rows]
            shifted = score_ref[s, k : k + plan.rows]
            totals[s] = shifted if k == 0 else totals[s] + shifted
    forward, backward = totals
    flip = ones_where(iota((plan.rows, plan.rows), 0) + iota((plan.rows, plan.rows), 1) == plan.rows - 1)
    for _ in range(3):
        high = backward.astype(BF16)
        forward = forward + dot(flip, high)
        backward = backward - high.astype(F32)
    out_ref[...] = forward


def neighbour_ways(count, cores):
    ways = []
    for i in range(count):
        for c in range(cores):
            step = 1 if (i + c) % 2 == 0 else -1
            there = (i + step, c ^ 1) if 0 <= i + step < count else (i, c ^ 1)
            ways.append((i * cores + c, there[0] * cores + there[1]))
    return ways


def stay(array):
    return pltpu.with_memory_space_constraint(array, pltpu.HBM)


def shards(tokens, nuc_table, short_filter, mr_filter, head_weight):
    _, short_len, channels = short_filter.shape
    filters, taps = mr_filter.shape
    head_taps, _, outs = head_weight.shape
    plan = Plan(tokens.shape[0], short_len, taps, head_taps)
    vmem = pl.BlockSpec(memory_space=pltpu.VMEM)
    hbm = pl.BlockSpec(memory_space=pl.ANY)

    own = tokens.reshape(1, plan.rows)
    own_here, weights, turned, edges = pl.pallas_call(
        functools.partial(prepare, plan),
        out_shape=(
            jax.ShapeDtypeStruct(own.shape, own.dtype),
            jax.ShapeDtypeStruct((3, plan.depth, channels), BF16),
            jax.ShapeDtypeStruct(mr_filter.shape, F32),
            jax.ShapeDtypeStruct((up(plan.missing, 1) * SUB, channels), F32),
        ),
        in_specs=[hbm] * 4,
        out_specs=(vmem,) * 4,
        scratch_shapes=[
            pltpu.VMEM(nuc_table.shape, BF16),
            pltpu.VMEM(short_filter.shape, F32),
            pltpu.VMEM(mr_filter.shape, F32),
            pltpu.SemaphoreType.DMA((4,)),
        ],
        compiler_params=pltpu.CompilerParams(vmem_limit_bytes=16 * MIB),
        cost_estimate=pl.CostEstimate(flops=10**8, bytes_accessed=10**7, transcendentals=0),
        name="prepare",
    )(*(stay(a) for a in (own, nuc_table, short_filter, mr_filter)))

    count, cores = lax.axis_size("seq"), lax.axis_size("ch")
    ways = neighbour_ways(count, cores)
    one = lax.ppermute(own, ("seq", "ch"), ways)
    two = lax.ppermute(own, ("seq", "ch"), [(b, a) for a, b in ways])

    partial = pl.pallas_call(
        functools.partial(kernel, plan, count),
        out_shape=jax.ShapeDtypeStruct((plan.rows, outs), F32),
        in_specs=[vmem] * 6 + [hbm],
        out_specs=vmem,
        scratch_shapes=[
            pltpu.VMEM(head_weight.shape, BF16),
            pltpu.VMEM((STRANDS, plan.hot_rows, plan.depth), BF16),
            pltpu.VMEM((STRANDS, plan.track_rows, plan.depth), BF16),
            pltpu.VMEM((plan.mix_rows, plan.window), F32),
            pltpu.VMEM((2, WIDE * filters // channels * plan.mix_rows, plan.window), BF16),
            pltpu.VMEM((2, WIDE // HALF, plan.window, WIDE), BF16),
            pltpu.VMEM((2, STRANDS, PARTS, SUB, WIDE), F32),
            pltpu.VMEM((2, STRANDS, plan.track_rows, WIDE), F32),
            pltpu.VMEM((STRANDS * plan.track_rows, channels), BF16),
            pltpu.VMEM((STRANDS, plan.track_rows, outs), F32),
            pltpu.SemaphoreType.DMA,
        ],
        compiler_params=pltpu.CompilerParams(vmem_limit_bytes=24 * MIB),
        cost_estimate=pl.CostEstimate(flops=8 * 10**9, bytes_accessed=10**7, transcendentals=0),
        name="annotate",
    )(one, own_here, two, weights, turned, edges, stay(head_weight))

    ring = [(i, (i + 1) % cores) for i in range(cores)]
    total, moving = partial, partial
    for _ in range(cores - 1):
        moving = lax.ppermute(moving, "ch", ring)
        total = total + moving
    return total.astype(BF16)


def solution(mesh):
    in_specs = (
        P(("groups", "seq")),
        P(None, None, "ch"),
        P(None, None, "ch"),
        P("ch", None),
        P(None, "ch", None),
    )
    out_specs = P(("groups", "seq"), None)
    return jax.shard_map(shards, mesh=mesh, in_specs=in_specs, out_specs=out_specs, check_vma=False)
```

```python
import functools

import jax
import jax.numpy as jnp
from jax import lax
from jax.experimental import pallas as pl
from jax.experimental.pallas import tpu as pltpu
from jax.sharding import PartitionSpec as P

LANES = 128
HALF = 64
WIDE = 256
SUB = 8
PACK = 16
LETTERS = 4
STRANDS = 2
PARTS = 2
F32 = jnp.float32
BF16 = jnp.bfloat16
MIB = 1024 * 1024


def up(value, step):
    return -(-value // step) * step


def iota(shape, dim):
    return lax.broadcasted_iota(jnp.int32, shape, dim)


def dot(a, b):
    return jnp.dot(a, b, preferred_element_type=F32)


def ones_where(mask):
    return mask.astype(F32).astype(BF16)


class Plan:
    def __init__(self, rows, short_len, taps, head_taps):
        self.rows, self.short_len, self.taps, self.head_taps = rows, short_len, taps, head_taps
        self.rim = (head_taps - 1) // 2
        self.part = rows // PARTS
        self.window = 2 * taps
        self.offset = self.window - self.part - 2 * self.rim
        self.missing = taps - 1 - self.offset
        self.mix_rows = up(self.part + 2 * self.rim, SUB)
        self.track_rows = (PARTS - 1) * self.part + self.mix_rows
        self.hot_rows = PACK + (PARTS - 1) * self.part + self.window
        self.lead = PACK + self.offset + self.rim + short_len - 1
        self.query_lead = PACK + self.offset
        self.width = up(self.query_lead + self.track_rows + short_len, LANES)
        self.depth = 2 * LETTERS * up(short_len, 2)


def build_weights(plan, nuc_ref, sf_ref, wn_ref):
    row = iota((2 * LETTERS, WIDE), 0)
    first = row < LETTERS
    short_len = plan.short_len

    def step(v, carry):
        lanes = pl.ds(pl.multiple_of(v * WIDE, WIDE), WIDE)
        for m in range(3):
            nuc = nuc_ref[m, :, lanes].astype(F32)
            nuc = jnp.concatenate([nuc, nuc], axis=0)
            taps = sf_ref[m, :, lanes]
            pieces = []
            for lag in range(0, short_len, 2):
                a = jnp.broadcast_to(taps[lag : lag + 1], row.shape)
                if lag + 1 < short_len:
                    b = jnp.broadcast_to(taps[lag + 1 : lag + 2], row.shape)
                else:
                    b = jnp.zeros(row.shape, F32)
                pieces.append(jnp.where(first, a, b) * nuc)
            product = jnp.concatenate(pieces, axis=0)
            high = product.astype(BF16)
            low = (product - high.astype(F32)).astype(BF16)
            wn_ref[m, :, lanes] = jnp.concatenate([high, low], axis=0)
        return carry

    lax.fori_loop(0, nuc_ref.shape[2] // WIDE, step, 0)


def build_turned(plan, mr_ref, fr_ref):
    total = iota((plan.taps, plan.taps), 0) + iota((plan.taps, plan.taps), 1)
    turn = (total == plan.offset) | (total == plan.offset + plan.taps)
    fr_ref[...] = dot(mr_ref[...].astype(BF16), ones_where(turn))


def build_masks(plan, mask_ref):
    taps = plan.taps
    gap = iota((plan.mix_rows, taps), 0) - iota((plan.mix_rows, taps), 1)
    mask_ref[:, :taps] = ((gap <= plan.missing) & (gap >= -plan.offset)).astype(F32)
    mask_ref[:, taps:] = (gap > plan.missing).astype(F32)


def build_mixer(plan, taps_row, mask_ref):
    taps = plan.taps
    wide = jnp.broadcast_to(taps_row, (taps, taps))
    turned = pltpu.roll(wide, 0, 1, stride=1, stride_axis=0)
    turned = jnp.concatenate([turned, turned[: plan.mix_rows - taps]], axis=0)
    return (jnp.concatenate([turned, turned], axis=1) * mask_ref[...]).astype(BF16)


def build_edges(plan, mr_ref, edge_ref):
    filters, taps = mr_ref.shape
    channels = edge_ref.shape[1]
    rows = edge_ref.shape[0]
    row, tap = iota((rows, taps), 0), iota((rows, taps), 1)
    wanted = tap == row % SUB + plan.offset + 1 + row // SUB
    picked = lax.dot_general(
        ones_where(wanted), mr_ref[...].astype(BF16), (((1,), (1,)), ((), ())), preferred_element_type=F32
    ).astype(BF16)
    width = channels // filters

    def step(v, carry):
        shape = (filters, WIDE)
        spread = ones_where(iota(shape, 0) == (iota(shape, 1) + v * WIDE) // width)
        edge_ref[:, pl.ds(pl.multiple_of(v * WIDE, WIDE), WIDE)] = dot(picked, spread)
        return carry

    lax.fori_loop(0, channels // WIDE, step, 0)


def prepare(
    plan, own_hbm, nuc_hbm, sf_hbm, mr_hbm, own_ref, wn_ref, fr_ref, edge_ref,
    nuc_ref, sf_ref, mr_ref, sems,
):
    pairs = [(mr_hbm, mr_ref), (nuc_hbm, nuc_ref), (sf_hbm, sf_ref), (own_hbm, own_ref)]
    copies = [pltpu.make_async_copy(a, b, sems.at[i]) for i, (a, b) in enumerate(pairs)]
    for copy in copies:
        copy.start()
    copies[0].wait()
    build_turned(plan, mr_ref, fr_ref)
    build_edges(plan, mr_ref, edge_ref)
    for copy in copies[1:]:
        copy.wait()
    build_weights(plan, nuc_ref, sf_ref, wn_ref)


def coded_letters(plan, count, one_ref, own_ref, two_ref):
    place = lax.axis_index("seq")
    onward = lax.rem(place + lax.axis_index("ch"), 2) == 0
    one, two = one_ref[...], two_ref[...]
    before = jnp.where(onward, one, two) + 1
    after = jnp.where(onward, two, one) + 1
    before = jnp.where(place > 0, before, 0)
    after = jnp.where(place < count - 1, after, 0)
    around = jnp.concatenate([before, own_ref[...] + 1, after], axis=1)
    blocks = around.shape[1] // LANES
    pieces = [around[:, i * LANES : (i + 1) * LANES] for i in range(blocks)]
    pieces += [jnp.zeros_like(pieces[0])] * (up(blocks, SUB) - blocks)
    flip = ones_where(iota((LANES, LANES), 0) + iota((LANES, LANES), 1) == LANES - 1)
    turned = dot(jnp.concatenate(pieces, axis=0).astype(F32).astype(BF16), flip).astype(jnp.int32)
    back = jnp.concatenate([turned[i : i + 1] for i in reversed(range(blocks))], axis=1)
    back = jnp.where(back > 0, LETTERS + 1 - back, 0)
    rest = jnp.zeros((SUB - STRANDS, around.shape[1]), jnp.int32)
    return jnp.concatenate([around, back, rest], axis=0)


def build_onehot(plan, tok, hot_ref, query_ref):
    width = tok.shape[1]
    hot_lanes, query_lanes = up(plan.hot_rows, LANES), up(plan.track_rows, LANES)
    lags = []
    for lag in range(plan.short_len):
        lead = plan.rows - plan.lead + plan.short_len - 1 - lag
        a = pltpu.roll(tok, (width - lead) % width, 1)[:, :hot_lanes]
        b = pltpu.roll(tok, (width - lead - plan.query_lead) % width, 1)[:, :query_lanes]
        lags.append(jnp.concatenate([a, b], axis=1))
    own = lags[0] > 0
    zero = jnp.zeros_like(lags[0])
    lags = [jnp.where(own, lag, zero) for lag in lags]
    if len(lags) % 2:
        lags.append(zero)
    row = iota((2 * LETTERS, zero.shape[1]), 0)
    first = row < LETTERS
    letter = jnp.where(first, row, row - LETTERS) + 1
    for s in range(STRANDS):
        pieces = []
        for lag in range(0, len(lags), 2):
            a = jnp.broadcast_to(lags[lag][s : s + 1], row.shape)
            b = jnp.broadcast_to(lags[lag + 1][s : s + 1], row.shape)
            pieces.append((jnp.where(first, a, b) == letter).astype(F32))
        hot = jnp.concatenate(pieces + pieces, axis=0).T.astype(BF16)
        hot_ref[s] = hot[: plan.hot_rows]
        query_ref[s] = hot[hot_lanes : hot_lanes + plan.track_rows]


def kernel(
    plan, count, one_ref, own_ref, two_ref, wn_ref, fr_ref, edge_ref, hw_hbm, out_ref,
    hw_ref, hot_ref, query_ref, mask_ref, mixer_now, data_now, edge_now, query_now, track_ref, score_ref, sem,
):
    channels = wn_ref.shape[2]
    part, window, mix_rows = plan.part, plan.window, plan.mix_rows
    group_width = channels // fr_ref.shape[0]
    half_step = WIDE // group_width // 2
    tile_groups = HALF // group_width
    tile_rows = tile_groups * mix_rows

    fetch = pltpu.make_async_copy(hw_hbm, hw_ref, sem)
    fetch.start()
    build_masks(plan, mask_ref)
    tok = coded_letters(plan, count, one_ref, own_ref, two_ref)
    build_onehot(plan, tok, hot_ref, query_ref)

    lane_group = (iota((mix_rows, WIDE), 1) % HALF) // group_width
    low_half = iota((window, LANES), 1) < HALF
    low_mix = low_half[:mix_rows]

    steps = channels // WIDE

    def gate(v, slot, s):
        lanes = pl.ds(pl.multiple_of(v * WIDE, WIDE), WIDE)
        hot = hot_ref[s]
        gated = dot(hot, wn_ref[1, :, lanes]) * dot(hot, wn_ref[2, :, lanes])
        query_now[slot, s] = dot(query_ref[s], wn_ref[0, :, lanes])
        for p in range(PARTS):
            at = PACK + p * part
            edge_now[slot, s, p] = gated[at - SUB : at]
        for j in range(WIDE // LANES):
            some = slice(j * LANES, (j + 1) * LANES)
            a = gated[PACK : PACK + window, some]
            b = pltpu.roll(gated[PACK + part : PACK + part + window, some], HALF, 1)
            to = slice(s * LANES, (s + 1) * LANES)
            data_now[slot, 2 * j, :, to] = jnp.where(low_half, a, b).astype(BF16)
            data_now[slot, 2 * j + 1, :, to] = jnp.where(low_half, b, a).astype(BF16)

    def arrange(v, slot, i):
        first = pl.multiple_of((2 * v + i) * half_step, half_step)
        block = fr_ref[pl.ds(first, half_step), :]
        for g in range(half_step):
            at = (i * half_step + g) * mix_rows
            mixer_now[slot, at : at + mix_rows, :] = build_mixer(plan, block[g : g + 1], mask_ref)

    def mix(v, slot, j):
        some = slice(j * LANES, (j + 1) * LANES)
        to = pl.ds(pl.multiple_of(v * WIDE + j * LANES, LANES), LANES)
        mixed = []
        for h in range(2):
            at = (2 * j + h) * tile_rows
            mixers = mixer_now[slot, at : at + tile_rows, :]
            data = data_now[slot, 2 * j + h]
            middle = tile_rows // 2
            pieces = jnp.concatenate([dot(mixers[:middle], data), dot(mixers[middle:], data)], axis=0)
            chosen = pieces[:mix_rows]
            for g in range(1, tile_groups):
                chosen = jnp.where(lane_group == g, pieces[g * mix_rows : (g + 1) * mix_rows], chosen)
            mixed.append(chosen)
        for s in range(STRANDS):
            a, b = (m[:, s * LANES : (s + 1) * LANES] for m in mixed)
            both = [jnp.where(low_mix, a, b), pltpu.roll(jnp.where(low_mix, b, a), HALF, 1)]
            for p in range(PARTS):
                fix = both[p][:SUB]
                for d in range(plan.missing):
                    base = edge_now[slot, s, p, SUB - 1 - d : SUB - d, some]
                    fix = fix + edge_ref[d * SUB : (d + 1) * SUB, to] * base
                length = part if p < PARTS - 1 else mix_rows
                whole = jnp.concatenate([fix, both[p][SUB:length]], axis=0)
                own = query_now[slot, s, p * part : p * part + length, some]
                at = s * plan.track_rows + p * part
                track_ref[at : at + length, to] = (own * whole).astype(BF16)

    for s in range(STRANDS):
        gate(0, 0, s)
        arrange(0, 0, s)

    def both_slots(u, last):
        for slot in range(2):
            v = 2 * u + slot
            for i in range(2):
                if slot == 0 or not last:
                    gate(v + 1, 1 - slot, i)
                    arrange(v + 1, 1 - slot, i)
                mix(v, slot, i)

    def pair(u, carry):
        both_slots(u, False)
        return carry

    lax.fori_loop(0, steps // 2 - 1, pair, 0)
    both_slots(steps // 2 - 1, True)

    fetch.wait()
    totals = [None, None]
    for k in range(plan.head_taps):
        score = dot(track_ref[...], hw_ref[k])
        for s in range(STRANDS):
            score_ref[s] = score[s * plan.track_rows : (s + 1) * plan.track_rows]
            shifted = score_ref[s, k : k + plan.rows]
            totals[s] = shifted if k == 0 else totals[s] + shifted
    forward, backward = totals
    flip = ones_where(iota((plan.rows, plan.rows), 0) + iota((plan.rows, plan.rows), 1) == plan.rows - 1)
    for _ in range(3):
        high = backward.astype(BF16)
        forward = forward + dot(flip, high)
        backward = backward - high.astype(F32)
    out_ref[...] = forward


def neighbour_ways(count, cores):
    ways = []
    for i in range(count):
        for c in range(cores):
            step = 1 if (i + c) % 2 == 0 else -1
            there = (i + step, c ^ 1) if 0 <= i + step < count else (i, c ^ 1)
            ways.append((i * cores + c, there[0] * cores + there[1]))
    return ways


def stay(array):
    return pltpu.with_memory_space_constraint(array, pltpu.HBM)


def shards(tokens, nuc_table, short_filter, mr_filter, head_weight):
    _, short_len, channels = short_filter.shape
    filters, taps = mr_filter.shape
    head_taps, _, outs = head_weight.shape
    plan = Plan(tokens.shape[0], short_len, taps, head_taps)
    vmem = pl.BlockSpec(memory_space=pltpu.VMEM)
    hbm = pl.BlockSpec(memory_space=pl.ANY)

    own = tokens.reshape(1, plan.rows)
    own_here, weights, turned, edges = pl.pallas_call(
        functools.partial(prepare, plan),
        out_shape=(
            jax.ShapeDtypeStruct(own.shape, own.dtype),
            jax.ShapeDtypeStruct((3, plan.depth, channels), BF16),
            jax.ShapeDtypeStruct(mr_filter.shape, F32),
            jax.ShapeDtypeStruct((up(plan.missing, 1) * SUB, channels), F32),
        ),
        in_specs=[hbm] * 4,
        out_specs=(vmem,) * 4,
        scratch_shapes=[
            pltpu.VMEM(nuc_table.shape, BF16),
            pltpu.VMEM(short_filter.shape, F32),
            pltpu.VMEM(mr_filter.shape, F32),
            pltpu.SemaphoreType.DMA((4,)),
        ],
        compiler_params=pltpu.CompilerParams(vmem_limit_bytes=16 * MIB),
        cost_estimate=pl.CostEstimate(flops=10**8, bytes_accessed=10**7, transcendentals=0),
        name="prepare",
    )(*(stay(a) for a in (own, nuc_table, short_filter, mr_filter)))

    count, cores = lax.axis_size("seq"), lax.axis_size("ch")
    ways = neighbour_ways(count, cores)
    one = lax.ppermute(own, ("seq", "ch"), ways)
    two = lax.ppermute(own, ("seq", "ch"), [(b, a) for a, b in ways])

    partial = pl.pallas_call(
        functools.partial(kernel, plan, count),
        out_shape=jax.ShapeDtypeStruct((plan.rows, outs), F32),
        in_specs=[vmem] * 6 + [hbm],
        out_specs=vmem,
        scratch_shapes=[
            pltpu.VMEM(head_weight.shape, BF16),
            pltpu.VMEM((STRANDS, plan.hot_rows, plan.depth), BF16),
            pltpu.VMEM((STRANDS, plan.track_rows, plan.depth), BF16),
            pltpu.VMEM((plan.mix_rows, plan.window), F32),
            pltpu.VMEM((2, WIDE * filters // channels * plan.mix_rows, plan.window), BF16),
            pltpu.VMEM((2, WIDE // HALF, plan.window, WIDE), BF16),
            pltpu.VMEM((2, STRANDS, PARTS, SUB, WIDE), F32),
            pltpu.VMEM((2, STRANDS, plan.track_rows, WIDE), F32),
            pltpu.VMEM((STRANDS * plan.track_rows, channels), BF16),
            pltpu.VMEM((STRANDS, plan.track_rows, outs), F32),
            pltpu.SemaphoreType.DMA,
        ],
        compiler_params=pltpu.CompilerParams(vmem_limit_bytes=24 * MIB),
        cost_estimate=pl.CostEstimate(flops=8 * 10**9, bytes_accessed=10**7, transcendentals=0),
        name="annotate",
    )(one, own_here, two, weights, turned, edges, stay(head_weight))

    ring = [(i, (i + 1) % cores) for i in range(cores)]
    total, moving = partial, partial
    for _ in range(cores - 1):
        moving = lax.ppermute(moving, "ch", ring)
        total = total + moving
    return total.astype(BF16)


def solution(mesh):
    in_specs = (
        P(("groups", "seq")),
        P(None, None, "ch"),
        P(None, None, "ch"),
        P("ch", None),
        P(None, "ch", None),
    )
    out_specs = P(("groups", "seq"), None)
    return jax.shard_map(shards, mesh=mesh, in_specs=in_specs, out_specs=out_specs, check_vma=False)
```

```python
import functools

import jax
import jax.numpy as jnp
from jax import lax
from jax.experimental import pallas as pl
from jax.experimental.pallas import tpu as pltpu
from jax.sharding import PartitionSpec as P

LANES = 128
HALF = 64
WIDE = 256
SUB = 8
PACK = 16
LETTERS = 4
STRANDS = 2
PARTS = 2
F32 = jnp.float32
BF16 = jnp.bfloat16
MIB = 1024 * 1024


def up(value, step):
    return -(-value // step) * step


def iota(shape, dim):
    return lax.broadcasted_iota(jnp.int32, shape, dim)


def dot(a, b):
    return jnp.dot(a, b, preferred_element_type=F32)


def ones_where(mask):
    return mask.astype(F32).astype(BF16)


class Plan:
    def __init__(self, rows, short_len, taps, head_taps):
        self.rows, self.short_len, self.taps, self.head_taps = rows, short_len, taps, head_taps
        self.rim = (head_taps - 1) // 2
        self.part = rows // PARTS
        self.window = 2 * taps
        self.offset = self.window - self.part - 2 * self.rim
        self.missing = taps - 1 - self.offset
        self.mix_rows = up(self.part + 2 * self.rim, SUB)
        self.track_rows = (PARTS - 1) * self.part + self.mix_rows
        self.hot_rows = PACK + (PARTS - 1) * self.part + self.window
        self.lead = PACK + self.offset + self.rim + short_len - 1
        self.query_lead = PACK + self.offset
        self.width = up(self.query_lead + self.track_rows + short_len, LANES)
        self.depth = 2 * LETTERS * up(short_len, 2)


def build_weights(plan, nuc_ref, sf_ref, wn_ref):
    row = iota((2 * LETTERS, WIDE), 0)
    first = row < LETTERS
    short_len = plan.short_len

    def step(v, carry):
        lanes = pl.ds(pl.multiple_of(v * WIDE, WIDE), WIDE)
        for m in range(3):
            nuc = nuc_ref[m, :, lanes].astype(F32)
            nuc = jnp.concatenate([nuc, nuc], axis=0)
            taps = sf_ref[m, :, lanes]
            pieces = []
            for lag in range(0, short_len, 2):
                a = jnp.broadcast_to(taps[lag : lag + 1], row.shape)
                if lag + 1 < short_len:
                    b = jnp.broadcast_to(taps[lag + 1 : lag + 2], row.shape)
                else:
                    b = jnp.zeros(row.shape, F32)
                pieces.append(jnp.where(first, a, b) * nuc)
            product = jnp.concatenate(pieces, axis=0)
            high = product.astype(BF16)
            low = (product - high.astype(F32)).astype(BF16)
            wn_ref[m, :, lanes] = jnp.concatenate([high, low], axis=0)
        return carry

    lax.fori_loop(0, nuc_ref.shape[2] // WIDE, step, 0)


def build_turned(plan, mr_ref, fr_ref):
    total = iota((plan.taps, plan.taps), 0) + iota((plan.taps, plan.taps), 1)
    turn = (total == plan.offset) | (total == plan.offset + plan.taps)
    fr_ref[...] = dot(mr_ref[...].astype(BF16), ones_where(turn))


def build_masks(plan, mask_ref):
    taps = plan.taps
    gap = iota((plan.mix_rows, taps), 0) - iota((plan.mix_rows, taps), 1)
    mask_ref[:, :taps] = ((gap <= plan.missing) & (gap >= -plan.offset)).astype(F32)
    mask_ref[:, taps:] = (gap > plan.missing).astype(F32)


def build_mixer(plan, taps_row, mask_ref):
    taps = plan.taps
    wide = jnp.broadcast_to(taps_row, (taps, taps))
    turned = pltpu.roll(wide, 0, 1, stride=1, stride_axis=0)
    turned = jnp.concatenate([turned, turned[: plan.mix_rows - taps]], axis=0)
    near, far = turned * mask_ref[:, :taps], turned * mask_ref[:, taps:]
    return jnp.concatenate([near, far], axis=1).astype(BF16)


def build_edges(plan, mr_ref, edge_ref):
    filters, taps = mr_ref.shape
    channels = edge_ref.shape[1]
    rows = edge_ref.shape[0]
    row, tap = iota((rows, taps), 0), iota((rows, taps), 1)
    wanted = tap == row % SUB + plan.offset + 1 + row // SUB
    picked = lax.dot_general(
        ones_where(wanted), mr_ref[...].astype(BF16), (((1,), (1,)), ((), ())), preferred_element_type=F32
    ).astype(BF16)
    width = channels // filters

    def step(v, carry):
        shape = (filters, WIDE)
        spread = ones_where(iota(shape, 0) == (iota(shape, 1) + v * WIDE) // width)
        edge_ref[:, pl.ds(pl.multiple_of(v * WIDE, WIDE), WIDE)] = dot(picked, spread)
        return carry

    lax.fori_loop(0, channels // WIDE, step, 0)


def prepare(
    plan, own_hbm, nuc_hbm, sf_hbm, mr_hbm, own_ref, wn_ref, fr_ref, edge_ref,
    nuc_ref, sf_ref, mr_ref, sems,
):
    pairs = [(mr_hbm, mr_ref), (nuc_hbm, nuc_ref), (sf_hbm, sf_ref), (own_hbm, own_ref)]
    copies = [pltpu.make_async_copy(a, b, sems.at[i]) for i, (a, b) in enumerate(pairs)]
    for copy in copies:
        copy.start()
    copies[0].wait()
    build_turned(plan, mr_ref, fr_ref)
    build_edges(plan, mr_ref, edge_ref)
    for copy in copies[1:]:
        copy.wait()
    build_weights(plan, nuc_ref, sf_ref, wn_ref)


def coded_letters(plan, count, one_ref, own_ref, two_ref):
    place = lax.axis_index("seq")
    onward = lax.rem(place + lax.axis_index("ch"), 2) == 0
    one, two = one_ref[...], two_ref[...]
    before = jnp.where(onward, one, two) + 1
    after = jnp.where(onward, two, one) + 1
    before = jnp.where(place > 0, before, 0)
    after = jnp.where(place < count - 1, after, 0)
    around = jnp.concatenate([before, own_ref[...] + 1, after], axis=1)
    blocks = around.shape[1] // LANES
    pieces = [around[:, i * LANES : (i + 1) * LANES] for i in range(blocks)]
    pieces += [jnp.zeros_like(pieces[0])] * (up(blocks, SUB) - blocks)
    flip = ones_where(iota((LANES, LANES), 0) + iota((LANES, LANES), 1) == LANES - 1)
    turned = dot(jnp.concatenate(pieces, axis=0).astype(F32).astype(BF16), flip).astype(jnp.int32)
    back = jnp.concatenate([turned[i : i + 1] for i in reversed(range(blocks))], axis=1)
    back = jnp.where(back > 0, LETTERS + 1 - back, 0)
    rest = jnp.zeros((SUB - STRANDS, around.shape[1]), jnp.int32)
    return jnp.concatenate([around, back, rest], axis=0)


def build_onehot(plan, tok, hot_ref, query_ref):
    width = tok.shape[1]
    hot_lanes, query_lanes = up(plan.hot_rows, LANES), up(plan.track_rows, LANES)
    lags = []
    for lag in range(plan.short_len):
        lead = plan.rows - plan.lead + plan.short_len - 1 - lag
        a = pltpu.roll(tok, (width - lead) % width, 1)[:, :hot_lanes]
        b = pltpu.roll(tok, (width - lead - plan.query_lead) % width, 1)[:, :query_lanes]
        lags.append(jnp.concatenate([a, b], axis=1))
    own = lags[0] > 0
    zero = jnp.zeros_like(lags[0])
    lags = [jnp.where(own, lag, zero) for lag in lags]
    if len(lags) % 2:
        lags.append(zero)
    row = iota((2 * LETTERS, zero.shape[1]), 0)
    first = row < LETTERS
    letter = jnp.where(first, row, row - LETTERS) + 1
    for s in range(STRANDS):
        pieces = []
        for lag in range(0, len(lags), 2):
            a = jnp.broadcast_to(lags[lag][s : s + 1], row.shape)
            b = jnp.broadcast_to(lags[lag + 1][s : s + 1], row.shape)
            pieces.append((jnp.where(first, a, b) == letter).astype(F32))
        hot = jnp.concatenate(pieces + pieces, axis=0).T.astype(BF16)
        hot_ref[s] = hot[: plan.hot_rows]
        query_ref[s] = hot[hot_lanes : hot_lanes + plan.track_rows]


def kernel(
    plan, count, one_ref, own_ref, two_ref, wn_ref, fr_ref, edge_ref, hw_hbm, out_ref,
    hw_ref, hot_ref, query_ref, mask_ref, mixer_now, data_now, edge_now, query_now, track_ref, score_ref, sem,
):
    channels = wn_ref.shape[2]
    part, window, mix_rows = plan.part, plan.window, plan.mix_rows
    group_width = channels // fr_ref.shape[0]
    half_step = WIDE // group_width // 2
    tile_groups = HALF // group_width
    tile_rows = tile_groups * mix_rows

    fetch = pltpu.make_async_copy(hw_hbm, hw_ref, sem)
    fetch.start()
    build_masks(plan, mask_ref)
    tok = coded_letters(plan, count, one_ref, own_ref, two_ref)
    build_onehot(plan, tok, hot_ref, query_ref)

    lane_group = (iota((mix_rows, WIDE), 1) % HALF) // group_width
    low_half = iota((window, LANES), 1) < HALF
    low_mix = low_half[:mix_rows]

    steps = channels // WIDE

    def gate(v, slot, s):
        lanes = pl.ds(pl.multiple_of(v * WIDE, WIDE), WIDE)
        hot = hot_ref[s]
        gated = dot(hot, wn_ref[1, :, lanes]) * dot(hot, wn_ref[2, :, lanes])
        query_now[slot, s] = dot(query_ref[s], wn_ref[0, :, lanes])
        for p in range(PARTS):
            at = PACK + p * part
            edge_now[slot, s, p] = gated[at - SUB : at]
        for j in range(WIDE // LANES):
            some = slice(j * LANES, (j + 1) * LANES)
            a = gated[PACK : PACK + window, some]
            b = pltpu.roll(gated[PACK + part : PACK + part + window, some], HALF, 1)
            to = slice(s * LANES, (s + 1) * LANES)
            data_now[slot, 2 * j, :, to] = jnp.where(low_half, a, b).astype(BF16)
            data_now[slot, 2 * j + 1, :, to] = jnp.where(low_half, b, a).astype(BF16)

    def arrange(v, slot, i):
        first = pl.multiple_of((2 * v + i) * half_step, half_step)
        block = fr_ref[pl.ds(first, half_step), :]
        for g in range(half_step):
            at = (i * half_step + g) * mix_rows
            mixer_now[slot, at : at + mix_rows, :] = build_mixer(plan, block[g : g + 1], mask_ref)

    def mix(v, slot, j):
        some = slice(j * LANES, (j + 1) * LANES)
        to = pl.ds(pl.multiple_of(v * WIDE + j * LANES, LANES), LANES)
        mixed = []
        for h in range(2):
            at = (2 * j + h) * tile_rows
            mixers = mixer_now[slot, at : at + tile_rows, :]
            data = data_now[slot, 2 * j + h]
            middle = tile_rows // 2
            pieces = jnp.concatenate([dot(mixers[:middle], data), dot(mixers[middle:], data)], axis=0)
            chosen = pieces[:mix_rows]
            for g in range(1, tile_groups):
                chosen = jnp.where(lane_group == g, pieces[g * mix_rows : (g + 1) * mix_rows], chosen)
            mixed.append(chosen)
        for s in range(STRANDS):
            a, b = (m[:, s * LANES : (s + 1) * LANES] for m in mixed)
            both = [jnp.where(low_mix, a, b), pltpu.roll(jnp.where(low_mix, b, a), HALF, 1)]
            for p in range(PARTS):
                fix = both[p][:SUB]
                for d in range(plan.missing):
                    base = edge_now[slot, s, p, SUB - 1 - d : SUB - d, some]
                    fix = fix + edge_ref[d * SUB : (d + 1) * SUB, to] * base
                length = part if p < PARTS - 1 else mix_rows
                whole = jnp.concatenate([fix, both[p][SUB:length]], axis=0)
                own = query_now[slot, s, p * part : p * part + length, some]
                at = s * plan.track_rows + p * part
                track_ref[at : at + length, to] = (own * whole).astype(BF16)

    for s in range(STRANDS):
        gate(0, 0, s)
        arrange(0, 0, s)

    def both_slots(u, last):
        for slot in range(2):
            v = 2 * u + slot
            more = slot == 0 or not last
            if more:
                gate(v + 1, 1 - slot, 0)
                arrange(v + 1, 1 - slot, 0)
                gate(v + 1, 1 - slot, 1)
            mix(v, slot, 0)
            if more:
                arrange(v + 1, 1 - slot, 1)
            mix(v, slot, 1)

    def pair(u, carry):
        both_slots(u, False)
        return carry

    lax.fori_loop(0, steps // 2 - 1, pair, 0)
    both_slots(steps // 2 - 1, True)

    fetch.wait()
    totals = [None, None]
    for k in range(plan.head_taps):
        score = dot(track_ref[...], hw_ref[k])
        for s in range(STRANDS):
            score_ref[s] = score[s * plan.track_rows : (s + 1) * plan.track_rows]
            shifted = score_ref[s, k : k + plan.rows]
            totals[s] = shifted if k == 0 else totals[s] + shifted
    forward, backward = totals
    flip = ones_where(iota((plan.rows, plan.rows), 0) + iota((plan.rows, plan.rows), 1) == plan.rows - 1)
    for _ in range(3):
        high = backward.astype(BF16)
        forward = forward + dot(flip, high)
        backward = backward - high.astype(F32)
    out_ref[...] = forward


def neighbour_ways(count, cores):
    ways = []
    for i in range(count):
        for c in range(cores):
            step = 1 if (i + c) % 2 == 0 else -1
            there = (i + step, c ^ 1) if 0 <= i + step < count else (i, c ^ 1)
            ways.append((i * cores + c, there[0] * cores + there[1]))
    return ways


def stay(array):
    return pltpu.with_memory_space_constraint(array, pltpu.HBM)


def shards(tokens, nuc_table, short_filter, mr_filter, head_weight):
    _, short_len, channels = short_filter.shape
    filters, taps = mr_filter.shape
    head_taps, _, outs = head_weight.shape
    plan = Plan(tokens.shape[0], short_len, taps, head_taps)
    vmem = pl.BlockSpec(memory_space=pltpu.VMEM)
    hbm = pl.BlockSpec(memory_space=pl.ANY)

    own = tokens.reshape(1, plan.rows)
    own_here, weights, turned, edges = pl.pallas_call(
        functools.partial(prepare, plan),
        out_shape=(
            jax.ShapeDtypeStruct(own.shape, own.dtype),
            jax.ShapeDtypeStruct((3, plan.depth, channels), BF16),
            jax.ShapeDtypeStruct(mr_filter.shape, F32),
            jax.ShapeDtypeStruct((up(plan.missing, 1) * SUB, channels), F32),
        ),
        in_specs=[hbm] * 4,
        out_specs=(vmem,) * 4,
        scratch_shapes=[
            pltpu.VMEM(nuc_table.shape, BF16),
            pltpu.VMEM(short_filter.shape, F32),
            pltpu.VMEM(mr_filter.shape, F32),
            pltpu.SemaphoreType.DMA((4,)),
        ],
        compiler_params=pltpu.CompilerParams(vmem_limit_bytes=16 * MIB),
        cost_estimate=pl.CostEstimate(flops=10**8, bytes_accessed=10**7, transcendentals=0),
        name="prepare",
    )(*(stay(a) for a in (own, nuc_table, short_filter, mr_filter)))

    count, cores = lax.axis_size("seq"), lax.axis_size("ch")
    ways = neighbour_ways(count, cores)
    one = lax.ppermute(own, ("seq", "ch"), ways)
    two = lax.ppermute(own, ("seq", "ch"), [(b, a) for a, b in ways])

    partial = pl.pallas_call(
        functools.partial(kernel, plan, count),
        out_shape=jax.ShapeDtypeStruct((plan.rows, outs), F32),
        in_specs=[vmem] * 6 + [hbm],
        out_specs=vmem,
        scratch_shapes=[
            pltpu.VMEM(head_weight.shape, BF16),
            pltpu.VMEM((STRANDS, plan.hot_rows, plan.depth), BF16),
            pltpu.VMEM((STRANDS, plan.track_rows, plan.depth), BF16),
            pltpu.VMEM((plan.mix_rows, plan.window), F32),
            pltpu.VMEM((2, WIDE * filters // channels * plan.mix_rows, plan.window), BF16),
            pltpu.VMEM((2, WIDE // HALF, plan.window, WIDE), BF16),
            pltpu.VMEM((2, STRANDS, PARTS, SUB, WIDE), F32),
            pltpu.VMEM((2, STRANDS, plan.track_rows, WIDE), F32),
            pltpu.VMEM((STRANDS * plan.track_rows, channels), BF16),
            pltpu.VMEM((STRANDS, plan.track_rows, outs), F32),
            pltpu.SemaphoreType.DMA,
        ],
        compiler_params=pltpu.CompilerParams(vmem_limit_bytes=24 * MIB),
        cost_estimate=pl.CostEstimate(flops=8 * 10**9, bytes_accessed=10**7, transcendentals=0),
        name="annotate",
    )(one, own_here, two, weights, turned, edges, stay(head_weight))

    ring = [(i, (i + 1) % cores) for i in range(cores)]
    total, moving = partial, partial
    for _ in range(cores - 1):
        moving = lax.ppermute(moving, "ch", ring)
        total = total + moving
    return total.astype(BF16)


def solution(mesh):
    in_specs = (
        P(("groups", "seq")),
        P(None, None, "ch"),
        P(None, None, "ch"),
        P("ch", None),
        P(None, "ch", None),
    )
    out_specs = P(("groups", "seq"), None)
    return jax.shard_map(shards, mesh=mesh, in_specs=in_specs, out_specs=out_specs, check_vma=False)
```

```python
import functools

import jax
import jax.numpy as jnp
from jax import lax
from jax.experimental import pallas as pl
from jax.experimental.pallas import tpu as pltpu
from jax.sharding import PartitionSpec as P

LANES = 128
HALF = 64
WIDE = 256
SUB = 8
PACK = 16
LETTERS = 4
STRANDS = 2
PARTS = 2
F32 = jnp.float32
BF16 = jnp.bfloat16
MIB = 1024 * 1024


def up(value, step):
    return -(-value // step) * step


def iota(shape, dim):
    return lax.broadcasted_iota(jnp.int32, shape, dim)


def dot(a, b):
    return jnp.dot(a, b, preferred_element_type=F32)


def ones_where(mask):
    return mask.astype(F32).astype(BF16)


class Plan:
    def __init__(self, rows, short_len, taps, head_taps):
        self.rows, self.short_len, self.taps, self.head_taps = rows, short_len, taps, head_taps
        self.rim = (head_taps - 1) // 2
        self.part = rows // PARTS
        self.window = 2 * taps
        self.offset = self.window - self.part - 2 * self.rim
        self.missing = taps - 1 - self.offset
        self.mix_rows = up(self.part + 2 * self.rim, SUB)
        self.track_rows = (PARTS - 1) * self.part + self.mix_rows
        self.hot_rows = PACK + (PARTS - 1) * self.part + self.window
        self.lead = PACK + self.offset + self.rim + short_len - 1
        self.query_lead = PACK + self.offset
        self.width = up(self.query_lead + self.track_rows + short_len, LANES)
        self.depth = 2 * LETTERS * up(short_len, 2)


def build_weights(plan, nuc_ref, sf_ref, wn_ref):
    row = iota((2 * LETTERS, WIDE), 0)
    first = row < LETTERS
    short_len = plan.short_len

    def step(v, carry):
        lanes = pl.ds(pl.multiple_of(v * WIDE, WIDE), WIDE)
        for m in range(3):
            nuc = nuc_ref[m, :, lanes].astype(F32)
            nuc = jnp.concatenate([nuc, nuc], axis=0)
            taps = sf_ref[m, :, lanes]
            pieces = []
            for lag in range(0, short_len, 2):
                a = jnp.broadcast_to(taps[lag : lag + 1], row.shape)
                if lag + 1 < short_len:
                    b = jnp.broadcast_to(taps[lag + 1 : lag + 2], row.shape)
                else:
                    b = jnp.zeros(row.shape, F32)
                pieces.append(jnp.where(first, a, b) * nuc)
            product = jnp.concatenate(pieces, axis=0)
            high = product.astype(BF16)
            low = (product - high.astype(F32)).astype(BF16)
            wn_ref[m, :, lanes] = jnp.concatenate([high, low], axis=0)
        return carry

    lax.fori_loop(0, nuc_ref.shape[2] // WIDE, step, 0)


def build_turned(plan, mr_ref, fr_ref):
    total = iota((plan.taps, plan.taps), 0) + iota((plan.taps, plan.taps), 1)
    turn = (total == plan.offset) | (total == plan.offset + plan.taps)
    fr_ref[...] = dot(mr_ref[...].astype(BF16), ones_where(turn))


def build_masks(plan, mask_ref):
    taps = plan.taps
    gap = iota((plan.mix_rows, taps), 0) - iota((plan.mix_rows, taps), 1)
    mask_ref[:, :taps] = ((gap <= plan.missing) & (gap >= -plan.offset)).astype(F32)
    mask_ref[:, taps:] = (gap > plan.missing).astype(F32)


def build_mixer(plan, taps_row, mask_ref):
    taps = plan.taps
    wide = jnp.broadcast_to(taps_row, (taps, taps))
    turned = pltpu.roll(wide, 0, 1, stride=1, stride_axis=0)
    turned = jnp.concatenate([turned, turned[: plan.mix_rows - taps]], axis=0)
    near, far = turned * mask_ref[:, :taps], turned * mask_ref[:, taps:]
    return jnp.concatenate([near, far], axis=1).astype(BF16)


def build_edges(plan, mr_ref, edge_ref):
    filters, taps = mr_ref.shape
    channels = edge_ref.shape[1]
    rows = edge_ref.shape[0]
    row, tap = iota((rows, taps), 0), iota((rows, taps), 1)
    wanted = tap == row % SUB + plan.offset + 1 + row // SUB
    picked = lax.dot_general(
        ones_where(wanted), mr_ref[...].astype(BF16), (((1,), (1,)), ((), ())), preferred_element_type=F32
    ).astype(BF16)
    width = channels // filters

    def step(v, carry):
        shape = (filters, WIDE)
        spread = ones_where(iota(shape, 0) == (iota(shape, 1) + v * WIDE) // width)
        edge_ref[:, pl.ds(pl.multiple_of(v * WIDE, WIDE), WIDE)] = dot(picked, spread)
        return carry

    lax.fori_loop(0, channels // WIDE, step, 0)


def prepare(
    plan, own_hbm, nuc_hbm, sf_hbm, mr_hbm, own_ref, wn_ref, fr_ref, edge_ref,
    nuc_ref, sf_ref, mr_ref, sems,
):
    pairs = [(mr_hbm, mr_ref), (nuc_hbm, nuc_ref), (sf_hbm, sf_ref), (own_hbm, own_ref)]
    copies = [pltpu.make_async_copy(a, b, sems.at[i]) for i, (a, b) in enumerate(pairs)]
    for copy in copies:
        copy.start()
    copies[0].wait()
    build_turned(plan, mr_ref, fr_ref)
    build_edges(plan, mr_ref, edge_ref)
    for copy in copies[1:]:
        copy.wait()
    build_weights(plan, nuc_ref, sf_ref, wn_ref)


def coded_letters(plan, count, one_ref, own_ref, two_ref):
    place = lax.axis_index("seq")
    onward = lax.rem(place + lax.axis_index("ch"), 2) == 0
    one, two = one_ref[...], two_ref[...]
    before = jnp.where(onward, one, two) + 1
    after = jnp.where(onward, two, one) + 1
    before = jnp.where(place > 0, before, 0)
    after = jnp.where(place < count - 1, after, 0)
    around = jnp.concatenate([before, own_ref[...] + 1, after], axis=1)
    blocks = around.shape[1] // LANES
    pieces = [around[:, i * LANES : (i + 1) * LANES] for i in range(blocks)]
    pieces += [jnp.zeros_like(pieces[0])] * (up(blocks, SUB) - blocks)
    flip = ones_where(iota((LANES, LANES), 0) + iota((LANES, LANES), 1) == LANES - 1)
    turned = dot(jnp.concatenate(pieces, axis=0).astype(F32).astype(BF16), flip).astype(jnp.int32)
    back = jnp.concatenate([turned[i : i + 1] for i in reversed(range(blocks))], axis=1)
    back = jnp.where(back > 0, LETTERS + 1 - back, 0)
    rest = jnp.zeros((SUB - STRANDS, around.shape[1]), jnp.int32)
    return jnp.concatenate([around, back, rest], axis=0)


def build_onehot(plan, tok, hot_ref, query_ref):
    width = tok.shape[1]
    hot_lanes, query_lanes = up(plan.hot_rows, LANES), up(plan.track_rows, LANES)
    lags = []
    for lag in range(plan.short_len):
        lead = plan.rows - plan.lead + plan.short_len - 1 - lag
        a = pltpu.roll(tok, (width - lead) % width, 1)[:, :hot_lanes]
        b = pltpu.roll(tok, (width - lead - plan.query_lead) % width, 1)[:, :query_lanes]
        lags.append(jnp.concatenate([a, b], axis=1))
    own = lags[0] > 0
    zero = jnp.zeros_like(lags[0])
    lags = [jnp.where(own, lag, zero) for lag in lags]
    if len(lags) % 2:
        lags.append(zero)
    row = iota((2 * LETTERS, zero.shape[1]), 0)
    first = row < LETTERS
    letter = jnp.where(first, row, row - LETTERS) + 1
    for s in range(STRANDS):
        pieces = []
        for lag in range(0, len(lags), 2):
            a = jnp.broadcast_to(lags[lag][s : s + 1], row.shape)
            b = jnp.broadcast_to(lags[lag + 1][s : s + 1], row.shape)
            pieces.append((jnp.where(first, a, b) == letter).astype(F32))
        hot = jnp.concatenate(pieces + pieces, axis=0).T.astype(BF16)
        hot_ref[s] = hot[: plan.hot_rows]
        query_ref[s] = hot[hot_lanes : hot_lanes + plan.track_rows]


def kernel(
    plan, count, one_ref, own_ref, two_ref, wn_ref, fr_ref, edge_ref, hw_hbm, out_ref,
    hw_ref, hot_ref, query_ref, mask_ref, mixer_now, data_now, edge_now, query_now, track_ref, score_ref, sem,
):
    channels = wn_ref.shape[2]
    part, window, mix_rows = plan.part, plan.window, plan.mix_rows
    group_width = channels // fr_ref.shape[0]
    half_step = WIDE // group_width // 2
    tile_groups = HALF // group_width
    tile_rows = tile_groups * mix_rows

    fetch = pltpu.make_async_copy(hw_hbm, hw_ref, sem)
    fetch.start()
    build_masks(plan, mask_ref)
    tok = coded_letters(plan, count, one_ref, own_ref, two_ref)
    build_onehot(plan, tok, hot_ref, query_ref)

    lane_group = (iota((mix_rows, WIDE), 1) % HALF) // group_width
    low_half = iota((window, LANES), 1) < HALF
    low_mix = low_half[:mix_rows]

    steps = channels // WIDE

    def gate(v, slot, s):
        lanes = pl.ds(pl.multiple_of(v * WIDE, WIDE), WIDE)
        hot = hot_ref[s]
        gated = dot(hot, wn_ref[1, :, lanes]) * dot(hot, wn_ref[2, :, lanes])
        query_now[slot, s] = dot(query_ref[s], wn_ref[0, :, lanes])
        for p in range(PARTS):
            at = PACK + p * part
            edge_now[slot, s, p] = gated[at - SUB : at]
        for j in range(WIDE // LANES):
            some = slice(j * LANES, (j + 1) * LANES)
            a = gated[PACK : PACK + window, some]
            b = pltpu.roll(gated[PACK + part : PACK + part + window, some], HALF, 1)
            to = slice(s * LANES, (s + 1) * LANES)
            data_now[slot, 2 * j, :, to] = jnp.where(low_half, a, b).astype(BF16)
            data_now[slot, 2 * j + 1, :, to] = jnp.where(low_half, b, a).astype(BF16)

    def arrange(v, slot, i):
        first = pl.multiple_of((2 * v + i) * half_step, half_step)
        block = fr_ref[pl.ds(first, half_step), :]
        for g in range(half_step):
            at = (i * half_step + g) * mix_rows
            mixer_now[slot, at : at + mix_rows, :] = build_mixer(plan, block[g : g + 1], mask_ref)

    def mix(v, slot, j):
        some = slice(j * LANES, (j + 1) * LANES)
        to = pl.ds(pl.multiple_of(v * WIDE + j * LANES, LANES), LANES)
        mixed = []
        for h in range(2):
            at = (2 * j + h) * tile_rows
            mixers = mixer_now[slot, at : at + tile_rows, :]
            data = data_now[slot, 2 * j + h]
            middle = tile_rows // 2
            pieces = jnp.concatenate([dot(mixers[:middle], data), dot(mixers[middle:], data)], axis=0)
            chosen = pieces[:mix_rows]
            for g in range(1, tile_groups):
                chosen = jnp.where(lane_group == g, pieces[g * mix_rows : (g + 1) * mix_rows], chosen)
            mixed.append(chosen)
        for s in range(STRANDS):
            a, b = (m[:, s * LANES : (s + 1) * LANES] for m in mixed)
            both = [jnp.where(low_mix, a, b), pltpu.roll(jnp.where(low_mix, b, a), HALF, 1)]
            for p in range(PARTS):
                fix = both[p][:SUB]
                for d in range(plan.missing):
                    base = edge_now[slot, s, p, SUB - 1 - d : SUB - d, some]
                    fix = fix + edge_ref[d * SUB : (d + 1) * SUB, to] * base
                length = part if p < PARTS - 1 else mix_rows
                whole = jnp.concatenate([fix, both[p][SUB:length]], axis=0)
                own = query_now[slot, s, p * part : p * part + length, some]
                at = s * plan.track_rows + p * part
                track_ref[at : at + length, to] = (own * whole).astype(BF16)

    arrange(0, 0, 0)
    gate(0, 0, 0)
    gate(0, 0, 1)
    arrange(0, 0, 1)

    def both_slots(u, last):
        for slot in range(2):
            v = 2 * u + slot
            more = slot == 0 or not last
            if more:
                gate(v + 1, 1 - slot, 0)
                arrange(v + 1, 1 - slot, 0)
                gate(v + 1, 1 - slot, 1)
            mix(v, slot, 0)
            if more:
                arrange(v + 1, 1 - slot, 1)
            mix(v, slot, 1)

    def pair(u, carry):
        both_slots(u, False)
        return carry

    lax.fori_loop(0, steps // 2 - 1, pair, 0)
    both_slots(steps // 2 - 1, True)

    fetch.wait()
    totals = [None, None]
    for k in range(plan.head_taps):
        score = dot(track_ref[...], hw_ref[k])
        for s in range(STRANDS):
            score_ref[s] = score[s * plan.track_rows : (s + 1) * plan.track_rows]
            shifted = score_ref[s, k : k + plan.rows]
            totals[s] = shifted if k == 0 else totals[s] + shifted
    forward, backward = totals
    flip = ones_where(iota((plan.rows, plan.rows), 0) + iota((plan.rows, plan.rows), 1) == plan.rows - 1)
    for _ in range(3):
        high = backward.astype(BF16)
        forward = forward + dot(flip, high)
        backward = backward - high.astype(F32)
    out_ref[...] = forward


def neighbour_ways(count, cores):
    ways = []
    for i in range(count):
        for c in range(cores):
            step = 1 if (i + c) % 2 == 0 else -1
            there = (i + step, c ^ 1) if 0 <= i + step < count else (i, c ^ 1)
            ways.append((i * cores + c, there[0] * cores + there[1]))
    return ways


def stay(array):
    return pltpu.with_memory_space_constraint(array, pltpu.HBM)


def shards(tokens, nuc_table, short_filter, mr_filter, head_weight):
    _, short_len, channels = short_filter.shape
    filters, taps = mr_filter.shape
    head_taps, _, outs = head_weight.shape
    plan = Plan(tokens.shape[0], short_len, taps, head_taps)
    vmem = pl.BlockSpec(memory_space=pltpu.VMEM)
    hbm = pl.BlockSpec(memory_space=pl.ANY)

    own = tokens.reshape(1, plan.rows)
    own_here, weights, turned, edges = pl.pallas_call(
        functools.partial(prepare, plan),
        out_shape=(
            jax.ShapeDtypeStruct(own.shape, own.dtype),
            jax.ShapeDtypeStruct((3, plan.depth, channels), BF16),
            jax.ShapeDtypeStruct(mr_filter.shape, F32),
            jax.ShapeDtypeStruct((up(plan.missing, 1) * SUB, channels), F32),
        ),
        in_specs=[hbm] * 4,
        out_specs=(vmem,) * 4,
        scratch_shapes=[
            pltpu.VMEM(nuc_table.shape, BF16),
            pltpu.VMEM(short_filter.shape, F32),
            pltpu.VMEM(mr_filter.shape, F32),
            pltpu.SemaphoreType.DMA((4,)),
        ],
        compiler_params=pltpu.CompilerParams(vmem_limit_bytes=16 * MIB),
        cost_estimate=pl.CostEstimate(flops=10**8, bytes_accessed=10**7, transcendentals=0),
        name="prepare",
    )(*(stay(a) for a in (own, nuc_table, short_filter, mr_filter)))

    count, cores = lax.axis_size("seq"), lax.axis_size("ch")
    ways = neighbour_ways(count, cores)
    one = lax.ppermute(own, ("seq", "ch"), ways)
    two = lax.ppermute(own, ("seq", "ch"), [(b, a) for a, b in ways])

    partial = pl.pallas_call(
        functools.partial(kernel, plan, count),
        out_shape=jax.ShapeDtypeStruct((plan.rows, outs), F32),
        in_specs=[vmem] * 6 + [hbm],
        out_specs=vmem,
        scratch_shapes=[
            pltpu.VMEM(head_weight.shape, BF16),
            pltpu.VMEM((STRANDS, plan.hot_rows, plan.depth), BF16),
            pltpu.VMEM((STRANDS, plan.track_rows, plan.depth), BF16),
            pltpu.VMEM((plan.mix_rows, plan.window), F32),
            pltpu.VMEM((2, WIDE * filters // channels * plan.mix_rows, plan.window), BF16),
            pltpu.VMEM((2, WIDE // HALF, plan.window, WIDE), BF16),
            pltpu.VMEM((2, STRANDS, PARTS, SUB, WIDE), F32),
            pltpu.VMEM((2, STRANDS, plan.track_rows, WIDE), F32),
            pltpu.VMEM((STRANDS * plan.track_rows, channels), BF16),
            pltpu.VMEM((STRANDS, plan.track_rows, outs), F32),
            pltpu.SemaphoreType.DMA,
        ],
        compiler_params=pltpu.CompilerParams(vmem_limit_bytes=24 * MIB),
        cost_estimate=pl.CostEstimate(flops=8 * 10**9, bytes_accessed=10**7, transcendentals=0),
        name="annotate",
    )(one, own_here, two, weights, turned, edges, stay(head_weight))

    ring = [(i, (i + 1) % cores) for i in range(cores)]
    total, moving = partial, partial
    for _ in range(cores - 1):
        moving = lax.ppermute(moving, "ch", ring)
        total = total + moving
    return total.astype(BF16)


def solution(mesh):
    in_specs = (
        P(("groups", "seq")),
        P(None, None, "ch"),
        P(None, None, "ch"),
        P("ch", None),
        P(None, "ch", None),
    )
    out_specs = P(("groups", "seq"), None)
    return jax.shard_map(shards, mesh=mesh, in_specs=in_specs, out_specs=out_specs, check_vma=False)
```
